32 devices in a mesh: gx: 4 (over x, core), gy: 4 (over z), gz: 2 (over y).
Axes of the slice: x: 2, y: 2, z: 4, core: 2. Of those that a mesh axis runs over, the one named last changes fastest.
Arguments:
- positions: float32 [3, 16384], P(None, ('gx', 'gy', 'gz')), may hold values from 0 to 4, as said below
- velocities: float32 [3, 16384], P(None, ('gx', 'gy', 'gz')), may hold values from -3 to 3
- star_mass: float32 [16384], P(('gx', 'gy', 'gz')), may hold values from 0.0009765625 to 0.00390625
- far_previous: float32 [3, 16384], P(None, ('gx', 'gy', 'gz')), may hold values from -6 to 6
- cell_index: int32 [16384], P(('gx', 'gy', 'gz')), may hold values from 0 to 15, as said below
- ghost_list: int32 [8192], P(('gx', 'gy', 'gz')), may hold values from 0 to 511, as said below
- block_index: int32 [512, 128], P(('gx', 'gy', 'gz')), may hold values from 0 to 7423, as said below
- block_owner: int32 [512, 1], P(('gx', 'gy', 'gz')), may hold values from 0 to 1; in each aligned block of 16 rows (0 to 15, 16 to 31, ...) at most 16 rows name the same one
- substeps: int32 [512], P(('gx', 'gy', 'gz')), may hold values from 1 to 8, as said below
Outputs:
- far_acc: float32 [3, 16384], P(None, ('gx', 'gy', 'gz'))
- block_state: float32 [6, 131072], P(None, ('gx', 'gy', 'gz'))
The draws below stay inside these ranges and needn't reach their ends.
Inputs may be any that keep to these rules, and one draw needn't show every extreme that they name: `positions`: stars of the domain with coordinates (a, b, c) lie inside the unit box whose lowest corner is (a, b, c). `cell_index`: each cell of a domain is a box of a regular split of the domain's box, and holds at least 16 of its stars. `ghost_list`: A domain's 256 entries are distinct. `block_index`: each block's 128 entries are distinct pool columns of stars around one of the domain's own stars; no entry is a column of the domain's own sent stars or of a domain outside the grid. `block_owner`: no more than 16 of one domain's blocks have the same owner; in every draw some domain gives exactly 16 blocks to one owner. Every domain has a block with 8 substeps.
All inputs are finite; a program needn't handle non-finite values.
Results may differ from the reference program's by a relative error of at most 0.0003.
Values sent between devices are 32-bit elements; how exact they have to be, the bound alone decides.
A program may use at most 64 MiB of HBM per device.

```python
import math
import jax
import jax.numpy as jnp
import numpy as np
from jax import lax

STAR_DEV = 512
CELLS = 16
GHOSTS = 256
BLOCK = 128
BLOCKS_DEV = 16
SUBMAX = 8
DOM_X = 4
DOM_Y = 4
DOM_Z = 2
DOMAINS = 32
STARS = 16384
CAP = 16
POOL = 7424
GHOST_ROWS = 8192
BLOCK_ROWS = 512
OUT_COLS = 131072
N_GZ = 2


grid_steps = 40


def cell_splits():
    power = int(CELLS).bit_length() - 1
    return (2 ** ((power + 2) // 3), 2 ** ((power + 1) // 3), 2 ** (power // 3))


def domain_coords():
    number = jnp.arange(DOMAINS, dtype=jnp.int32)
    return jnp.stack([number // (DOM_Y * DOM_Z), number // DOM_Z % DOM_Y, number % DOM_Z], axis=1).astype(jnp.int32)


def star_layout(key):
    keys = jax.random.split(jax.random.fold_in(key, 7101), 3)
    along_x, along_y, along_z = cell_splits()
    span = jnp.array([grid_steps // along_x, grid_steps // along_y, grid_steps // along_z], jnp.int32)
    home = jnp.arange(STAR_DEV, dtype=jnp.int32) % CELLS
    lower = jnp.stack([home // (along_y * along_z), home // along_z % along_y, home % along_z], axis=1) * span[None, :]
    anywhere = jax.random.randint(keys[0], (DOMAINS, STAR_DEV, 3), 0, grid_steps).astype(jnp.int32)
    inside = jax.random.randint(keys[1], (DOMAINS, STAR_DEV, 3), 0, grid_steps).astype(jnp.int32)
    placed = lower[None] + inside % span[None, None, :]
    first = (jnp.arange(STAR_DEV, dtype=jnp.int32) < STAR_DEV // 2)[None, :, None]
    mixed = jnp.where(first, placed, anywhere)
    order = jax.vmap(lambda single: jax.random.permutation(single, STAR_DEV))(jax.random.split(keys[2], DOMAINS))
    grid_point = jnp.take_along_axis(mixed, order[:, :, None].astype(jnp.int32), axis=1).astype(jnp.int32)
    scaled = grid_point // span[None, None, :]
    cells = scaled[:, :, 0] * (along_y * along_z) + scaled[:, :, 1] * along_z + scaled[:, :, 2]
    return (grid_point, cells.astype(jnp.int32))


def ghost_layout(key):
    grid_point, cells = star_layout(key)
    keys = jax.random.split(jax.random.fold_in(key, 7102), 2)
    edge = jnp.min(jnp.minimum(grid_point, grid_steps - 1 - grid_point), axis=2)
    ties = jax.vmap(lambda single: jax.random.permutation(single, STAR_DEV))(jax.random.split(keys[0], DOMAINS)).astype(jnp.int32)
    ranked = jnp.argsort(edge * STAR_DEV + ties, axis=1)[:, :GHOSTS].astype(jnp.int32)
    shuffle = jax.vmap(lambda single: jax.random.permutation(single, GHOSTS))(jax.random.split(keys[1], DOMAINS)).astype(jnp.int32)
    listed = jnp.take_along_axis(ranked, shuffle, axis=1)
    corner = jnp.argmin(jnp.sum(grid_point, axis=2) * STAR_DEV + ties, axis=1).astype(jnp.int32)
    column = jnp.arange(GHOSTS, dtype=jnp.int32)[None, :]
    found = jnp.min(jnp.where(listed == corner[:, None], column, GHOSTS - 1), axis=1)
    last = listed[:, GHOSTS - 1]
    listed = jnp.where(column == found[:, None], last[:, None], listed)
    listed = jnp.where(column == GHOSTS - 1, corner[:, None], listed)
    return (grid_point, listed.astype(jnp.int32))


def draw_cell_index(key, part):
    grid_point, cells = star_layout(key)
    return cells.reshape(STARS).astype(jnp.int32)


def draw_ghost_list(key, part):
    grid_point, listed = ghost_layout(key)
    return listed.reshape(GHOST_ROWS).astype(jnp.int32)


def draw_positions(key, part):
    grid_point, cells = star_layout(key)
    coords = domain_coords()
    whole = (grid_point + coords[:, None, :] * grid_steps).astype(jnp.float32)
    jitter_key = jax.random.fold_in(key, 7104)
    jitter = jnp.clip(0.2 * jax.random.normal(jitter_key, (DOMAINS, STAR_DEV, 3), jnp.float32), -0.45, 0.45)
    points = (whole + 0.5 + jitter) / float(grid_steps)
    return points.transpose(2, 0, 1).reshape(3, STARS).astype(jnp.float32)


def draw_block_index(key, part):
    grid_point, listed = ghost_layout(key)
    keys = jax.random.split(jax.random.fold_in(key, 7103), 3)
    coords = domain_coords()
    global_point = (grid_point + coords[:, None, :] * grid_steps).astype(jnp.int32)
    ghost_point = jnp.take_along_axis(global_point, listed[:, :, None], axis=1)
    padded = jnp.pad(ghost_point.reshape(DOM_X, DOM_Y, DOM_Z, GHOSTS, 3), ((1, 1), (1, 1), (1, 1), (0, 0), (0, 0)))
    present = jnp.pad(jnp.ones((DOM_X, DOM_Y, DOM_Z), jnp.int32), 1)
    middle_mark = (jnp.arange(27, dtype=jnp.int32) == 13).astype(jnp.int32).reshape(3, 3, 3)
    star_number = jnp.arange(STAR_DEV, dtype=jnp.int32)
    sums = jnp.sum(grid_point, axis=2) * STAR_DEV + star_number[None, :]
    upper = jnp.argmax(sums, axis=1).astype(jnp.int32)
    lower = jnp.argmin(sums, axis=1).astype(jnp.int32)
    random_centre = jax.random.randint(keys[0], (DOMAINS, BLOCKS_DEV), 0, STAR_DEV).astype(jnp.int32)
    slot = jnp.arange(BLOCKS_DEV, dtype=jnp.int32)[None, :]
    centres = jnp.where(slot == 0, 0, random_centre)
    centres = jnp.where(slot == 1, upper[:, None], centres)
    centres = jnp.where(slot == 2, lower[:, None], centres).astype(jnp.int32)
    limit = 3 * (3 * grid_steps) ** 2 + 1
    pool_number = jnp.arange(POOL, dtype=jnp.int32)
    forced = (jnp.arange(DOMAINS, dtype=jnp.int32)[:, None] == 0) & (slot == 1)
    tie_keys = jax.random.split(keys[1], DOMAINS)
    order_keys = jax.random.split(keys[2], DOMAINS)

    def one_domain(inputs):
        number, own, centre, force_row, tie_key, order_key = inputs
        first = number // (DOM_Y * DOM_Z)
        second = number // DOM_Z % DOM_Y
        third = number % DOM_Z
        nought = jnp.zeros((), jnp.int32)
        near = lax.dynamic_slice(padded, (first, second, third, nought, nought), (3, 3, 3, GHOSTS, 3)).reshape(27 * GHOSTS, 3)
        alive = lax.dynamic_slice(present, (first, second, third), (3, 3, 3)) * (1 - middle_mark)
        alive = jnp.broadcast_to(alive.reshape(27, 1), (27, GHOSTS)).reshape(27 * GHOSTS)
        pool_point = jnp.concatenate([own, near], axis=0)
        pool_live = jnp.concatenate([jnp.ones((STAR_DEV,), jnp.int32), alive])
        middle = own[centre]
        offset = pool_point[None, :, :] - middle[:, None, :]
        distance = jnp.sum(offset * offset, axis=2)
        distance = jnp.where(pool_live[None, :] > 0, distance, limit)
        distance = jnp.where(force_row[:, None] & (pool_number[None, :] == POOL - 1), 0, distance)
        ties = jax.vmap(lambda single: jax.random.permutation(single, POOL))(jax.random.split(tie_key, BLOCKS_DEV)).astype(jnp.int32)
        nearest = jnp.argsort(distance * POOL + ties, axis=1)[:, :BLOCK].astype(jnp.int32)
        shuffle = jax.vmap(lambda single: jax.random.permutation(single, BLOCK))(jax.random.split(order_key, BLOCKS_DEV)).astype(jnp.int32)
        return jnp.take_along_axis(nearest, shuffle, axis=1).astype(jnp.int32)
    numbers = jnp.arange(DOMAINS, dtype=jnp.int32)
    chosen = lax.map(one_domain, (numbers, global_point, centres, forced, tie_keys, order_keys))
    return chosen.reshape(BLOCK_ROWS, BLOCK).astype(jnp.int32)


def draw_substeps(key, part):
    base = jax.random.fold_in(key, 7003)
    keys = jax.random.split(base, 2)
    counts = jax.random.randint(keys[0], (DOMAINS, BLOCKS_DEV), 1, SUBMAX + 1)
    chosen = jax.random.randint(keys[1], (DOMAINS, 1), 0, BLOCKS_DEV)
    counts = jnp.where(jnp.arange(BLOCKS_DEV)[None, :] == chosen, SUBMAX, counts)
    return counts.reshape(BLOCK_ROWS).astype(jnp.int32)


def block_levels(rng, extent, cuts, smallest, top_value):
    gain = 1.0
    for axis_at, parts in cuts:
        steps = jax.random.uniform(jax.random.fold_in(jax.random.fold_in(rng, 6), axis_at), (parts,), jnp.float32, smallest / len(cuts), top_value / len(cuts))
        gain = gain * jnp.repeat(jnp.exp(steps), extent[axis_at] // parts).reshape((-1,) + (1,) * (len(extent) - 1 - axis_at))
    return gain


def assign_block(key, own, number, rows, count, top, most, slope):
    ranking = jax.random.permutation(key, count)
    crowded, usual = shares(count, rows * top, most, slope, True), shares(count, rows * top, most, slope, False)
    places = jnp.arange(count)

    def named(lengths, offset_by):
        used = int((lengths > 0).sum())
        fixed = max(1, used // 4)
        passed = fixed + (places - fixed + offset_by * (used - fixed)) % max(1, count - fixed)
        return jnp.zeros((count,), jnp.int32).at[ranking[jnp.where(places < fixed, places, passed)]].set(jnp.asarray(lengths, jnp.int32))

    lengths = jnp.where(number % 4 == 0, named(crowded, number // 4), named(usual, number - number // 4 - 1))
    mixed = jax.random.permutation(jax.random.fold_in(own, 3), count)
    donor, sink = mixed[0:count // 2 * 2:2], mixed[1:count // 2 * 2:2]
    room = jnp.minimum(lengths[donor] - 1, most - lengths[sink]) // 2
    room = jnp.where((donor == ranking[0]) | (sink == ranking[0]) | (lengths[sink] == 0), 0, jnp.maximum(room, 0))
    passed = jax.random.randint(jax.random.fold_in(own, 4), (count // 2,), 0, 1 << 20) % (room + 1)
    lengths = lengths.at[donor].add(-passed).at[sink].add(passed)
    items = jnp.searchsorted(jnp.cumsum(lengths), jnp.arange(rows * top), side="right").astype(jnp.int32)
    listing = items.reshape(top, rows).T
    listing = listing[jax.random.permutation(jax.random.fold_in(own, 1), rows)]
    offset_by = jax.random.randint(jax.random.fold_in(own, 2), (rows, 1), 0, top)
    return jnp.take_along_axis(listing, (jnp.arange(top)[None, :] + offset_by) % top, axis=1)


def shares(amount, total, reach, lean, full):
    loads = [(1 << 20) // math.isqrt(standing ** lean) + 1 for standing in range(1, amount + 1)]
    largest = reach if full else min(reach, max(-(-total // amount), total * loads[0] // sum(loads)))
    least = 1 if total - largest >= amount - 1 else 0
    holding, rest = [largest] + [least] * (amount - 1), total - largest - least * (amount - 1)
    while rest > 0:
        candidates = [i for i in range(1, amount) if holding[i] < largest] or [i for i in range(1, amount) if holding[i] < reach]
        whole, left = sum([loads[i] for i in candidates]), rest
        for i in candidates:
            addition = min(reach - holding[i], max(1, left * loads[i] // whole), rest)
            holding[i] = holding[i] + addition
            rest = rest - addition
    return np.array(holding)


def scatter_about(stream_key, shape, deviation, reach, pieces=(), kind=jnp.bfloat16):
    result = deviation * jax.random.normal(stream_key, shape, jnp.float32)
    if pieces:
        result = result * block_levels(stream_key, shape, pieces, -0.22, 0.18)
    return jnp.clip(result, -reach, reach).astype(kind)


def setup_inputs(seed: int = 0) -> dict:
    arg_keys = jax.random.split(jax.random.key(seed), 10)
    positions = draw_positions(jax.random.fold_in(arg_keys[9], 71), 0)
    velocities = scatter_about(arg_keys[1], (3, STARS), 0.5, 3.0, ((1, 32),), jnp.float32)
    star_mass = jnp.clip(jnp.exp(math.log(0.00390625) - 1.3862944 * jax.random.uniform(arg_keys[2], (STARS,), jnp.float32) ** block_levels(arg_keys[2], (STARS,), ((0, 32),), -0.2, 0.2)), 0.0009765625, 0.00390625)
    far_previous = scatter_about(arg_keys[3], (3, STARS), 1.0, 6.0, ((1, 32),), jnp.float32)
    cell_index = draw_cell_index(jax.random.fold_in(arg_keys[9], 71), 0)
    ghost_list = draw_ghost_list(jax.random.fold_in(arg_keys[9], 71), 0)
    block_index = draw_block_index(jax.random.fold_in(arg_keys[9], 71), 0)
    block_owner_keys = jax.random.split(jax.random.fold_in(arg_keys[7], 1), BLOCK_ROWS // BLOCKS_DEV)
    block_owner_turns = jax.random.permutation(jax.random.fold_in(arg_keys[7], 3), BLOCK_ROWS // BLOCKS_DEV)
    block_owner = jax.vmap(lambda own, number: assign_block(jax.random.fold_in(arg_keys[7], 2), own, number, BLOCKS_DEV, N_GZ, 1, CAP, 2))(block_owner_keys, block_owner_turns).reshape((BLOCK_ROWS, 1))
    substeps = draw_substeps(jax.random.fold_in(arg_keys[9], 71), 0)
    return {"positions": positions, "velocities": velocities, "star_mass": star_mass, "far_previous": far_previous, "cell_index": cell_index, "ghost_list": ghost_list, "block_index": block_index, "block_owner": block_owner, "substeps": substeps}


SOFTENING = 0.0025
INNER_RADIUS = 0.25
OUTER_RADIUS = 1.0
TIME_STEP = 0.25

def changeover(radius):
    fraction = jnp.clip((radius - INNER_RADIUS) / (OUTER_RADIUS - INNER_RADIUS), 0.0, 1.0)
    return 1.0 - fraction * fraction * (3.0 - 2.0 * fraction)

def evaluate(position, velocity, masses):
    offset = position[:, :, None, :] - position[:, :, :, None]
    relative = velocity[:, :, None, :] - velocity[:, :, :, None]
    square = lax.optimization_barrier(jnp.sum(offset * offset, axis=0)) + SOFTENING
    radius = jnp.sqrt(square)
    weight = masses[:, None, :] * changeover(radius) / (square * radius)
    radial_rate = lax.optimization_barrier(jnp.sum(offset * relative, axis=0)) / square
    acceleration = lax.optimization_barrier(jnp.sum(weight[None] * offset, axis=-1))
    jerk_term = lax.optimization_barrier(jnp.sum(weight[None] * (relative - 3.0 * radial_rate[None] * offset), axis=-1))
    return (acceleration, jerk_term)

def integrate(state, step_count):
    start_position = state[0:3]
    start_velocity = state[3:6]
    position = start_position
    velocity = start_velocity
    masses = state[6]
    widths = (TIME_STEP / jnp.maximum(step_count, 1.0))[None, :, None]
    squared = widths * widths
    acc_old, jerk_old = evaluate(position, velocity, masses)
    for number in range(SUBMAX):
        live = (step_count > number)[None, :, None]
        predicted = position + widths * velocity + 0.5 * squared * acc_old + squared * widths / 6.0 * jerk_old
        predicted_vel = velocity + widths * acc_old + 0.5 * squared * jerk_old
        acc_new, jerk_new = evaluate(predicted, predicted_vel, masses)
        velocity_new = velocity + 0.5 * widths * (acc_old + acc_new) + squared / 12.0 * (jerk_old - jerk_new)
        position_new = position + 0.5 * widths * (velocity + velocity_new) + squared / 12.0 * (acc_old - acc_new)
        position = jnp.where(live, position_new, position)
        velocity = jnp.where(live, velocity_new, velocity)
        acc_old = jnp.where(live, acc_new, acc_old)
        jerk_old = jnp.where(live, jerk_new, jerk_old)
    return jnp.concatenate([position - start_position, velocity - start_velocity], axis=0)

def far_block(total, cells, stars):
    offset = cells[1:4, :, None] - stars[:, None, :]
    square = lax.optimization_barrier(jnp.sum(offset * offset, axis=0)) + SOFTENING
    radius = jnp.sqrt(square)
    weight = cells[0][:, None] * (1.0 - changeover(radius)) / (square * radius)
    return total + lax.optimization_barrier(jnp.sum(weight[None] * offset, axis=1))

def far_field(stars, cells):
    width = math.gcd(cells.shape[1], 512)
    blocks = cells.reshape(4, cells.shape[1] // width, width).transpose(1, 0, 2)

    def step(carry, piece):
        return (far_block(carry, piece, stars), None)
    total, unused = lax.scan(step, jnp.zeros_like(stars), blocks)
    return total

def reference(positions, velocities, star_mass, far_previous, cell_index, ghost_list, block_index, block_owner, substeps):
    star_number = jnp.arange(STARS, dtype=jnp.int32)
    segment = cell_index + star_number // STAR_DEV * CELLS
    cell_mass = jax.ops.segment_sum(star_mass, segment, DOMAINS * CELLS)
    weighted = jax.ops.segment_sum((positions * star_mass[None]).T, segment, DOMAINS * CELLS).T
    cells = jnp.concatenate([cell_mass[None], weighted / cell_mass[None]], axis=0)
    star_blocks = positions.reshape(3, DOMAINS, STAR_DEV).transpose(1, 0, 2)
    far_acc = lax.map(lambda stars: far_field(stars, cells), star_blocks)
    far_acc = far_acc.transpose(1, 0, 2).reshape(3, STARS)
    kicked = velocities + far_previous * (0.5 * TIME_STEP)
    local_rows = jnp.concatenate([positions, kicked, star_mass[None]], axis=0)
    local_rows = local_rows.reshape(7, DOMAINS, STAR_DEV).transpose(1, 0, 2)
    ghosts = jax.vmap(lambda rows, chosen: rows[:, chosen])(local_rows, ghost_list.reshape(DOMAINS, GHOSTS))
    grid = ghosts.reshape(DOM_X, DOM_Y, DOM_Z, 7, GHOSTS)
    padded = jnp.pad(grid, ((1, 1), (1, 1), (1, 1), (0, 0), (0, 0)))
    chosen_rows = block_index.reshape(DOMAINS, BLOCKS_DEV, BLOCK)
    counts = substeps.reshape(DOMAINS, BLOCKS_DEV).astype(jnp.float32)

    def one_domain(inputs):
        number, rows, chosen, step_count = inputs
        first = number // (DOM_Y * DOM_Z)
        second = number // DOM_Z % DOM_Y
        third = number % DOM_Z
        nought = jnp.zeros((), jnp.int32)
        near = lax.dynamic_slice(padded, (first, second, third, nought, nought), (3, 3, 3, 7, GHOSTS))
        near = near.transpose(3, 0, 1, 2, 4).reshape(7, 27 * GHOSTS)
        pool = jnp.concatenate([rows, near], axis=1)
        return integrate(pool[:, chosen], step_count)
    numbers = jnp.arange(DOMAINS, dtype=jnp.int32)
    results = lax.map(one_domain, (numbers, local_rows, chosen_rows, counts))
    owners = block_owner.reshape(DOMAINS, BLOCKS_DEV)
    marks = (owners[:, :, None] == jnp.arange(DOM_Z, dtype=jnp.int32)[None, None, :]).astype(jnp.int32)
    ranks = lax.optimization_barrier(jnp.sum((jnp.cumsum(marks, axis=1) - marks) * marks, axis=2))
    target = numbers[:, None] // DOM_Z * DOM_Z + owners
    source = jnp.broadcast_to(numbers[:, None] % DOM_Z, owners.shape)
    placed = jnp.zeros((DOMAINS, DOM_Z, CAP, 6, BLOCK), results.dtype)
    placed = placed.at[target, source, ranks].set(results.transpose(0, 2, 1, 3))
    block_state = placed.transpose(3, 0, 1, 2, 4).reshape(6, OUT_COLS)
    return (far_acc, block_state)
```

```python
import functools

import jax
import jax.numpy as jnp
from jax import lax
from jax.experimental import pallas as pl
from jax.experimental.pallas import tpu as pltpu
from jax.sharding import PartitionSpec as P

CELLS = 16
BLOCKS_DEV = 16
SUBMAX = 8
AXES = ("gx", "gy", "gz")
MESH = pl.DeviceIdType.MESH
LANES = 128

SOFTENING = 0.0025
INNER_RADIUS = 0.25
OUTER_RADIUS = 1.0
TIME_STEP = 0.25
SPAN = OUTER_RADIUS - INNER_RADIUS

BF16 = jnp.bfloat16
F32 = jnp.float32


def three(value):
    high = value.astype(BF16).astype(F32)
    rest = value - high
    middle = rest.astype(BF16).astype(F32)
    low = (rest - middle).astype(BF16).astype(F32)
    return high, middle, low


def pick(chunks, index):
    index = jnp.broadcast_to(index, (8, LANES))
    lane, chunk = index & (LANES - 1), index >> 7
    found = jnp.zeros((8, LANES), F32)
    for number, piece in chunks:
        found = jnp.where(chunk == number, jnp.take_along_axis(piece, lane, axis=1), found)
    return found


def prepare(pos_ref, vel_ref, mass_ref, far_ref, cell_ref, ghost_ref, rows_ref, sent_ref, moment_ref):
    stars = pos_ref.shape[1]
    position, mass = pos_ref[...], mass_ref[...]
    kicked = vel_ref[...] + far_ref[...] * (0.5 * TIME_STEP)
    rows = jnp.concatenate([position, kicked, mass, jnp.zeros((1, stars), F32)], axis=0)
    chunks = []
    for number in range(stars // LANES):
        piece = rows[:, number * LANES : (number + 1) * LANES]
        rows_ref[number] = piece
        chunks.append((number, piece))
    for number in range(ghost_ref.shape[1] // LANES):
        sent_ref[number] = pick(chunks, ghost_ref[:, number * LANES : (number + 1) * LANES])
    cell = lax.broadcasted_iota(jnp.int32, (LANES, stars), 0)
    member = jnp.where(jnp.broadcast_to(cell_ref[...], (LANES, stars)) == cell, 1.0, 0.0).astype(BF16)
    weighted = jnp.concatenate([mass, position * mass, jnp.zeros((4, stars), F32)], axis=0)
    parts = jnp.concatenate([*three(weighted), jnp.zeros_like(weighted)], axis=0).astype(BF16)
    sums = lax.dot_general(parts, member, (((1,), (1,)), ((), ())), preferred_element_type=F32)
    sums = sums[0:8] + sums[8:16] + sums[16:24]
    inside = lax.broadcasted_iota(jnp.int32, (1, LANES), 1) < CELLS
    total = jnp.where(inside, sums[0:1], 0.0)
    packed = total
    for axis in range(3):
        centre = jnp.where(inside, sums[axis + 1 : axis + 2] / jnp.where(inside, total, 1.0), 0.0)
        packed = packed + pltpu.roll(centre, (axis + 1) * CELLS, 1)
    moment_ref[0] = packed


def coordinates(sizes, number):
    return number // (sizes[1] * sizes[2]), number // sizes[2] % sizes[1], number % sizes[2]


def exchange(sizes, sent_ref, moment_ref, near_ref, every_ref, own_sem, moment_sems, send_sems, recv_sems):
    count = sizes[0] * sizes[1] * sizes[2]
    here = tuple(lax.axis_index(axis) for axis in AXES)
    me = (here[0] * sizes[1] + here[1]) * sizes[2] + here[2]
    barrier = pltpu.get_barrier_semaphore()

    def other(step):
        return coordinates(sizes, lax.rem(me + step, count))

    def greet(step, carry):
        pl.semaphore_signal(barrier, inc=1, device_id=other(step), device_id_type=MESH)
        return carry

    lax.fori_loop(1, count, greet, 0)
    own = pltpu.make_async_copy(moment_ref.at[0], every_ref.at[0], own_sem)
    own.start()
    pl.semaphore_wait(barrier, count - 1)

    def share(step, carry):
        pltpu.make_async_remote_copy(
            src_ref=moment_ref.at[0],
            dst_ref=every_ref.at[step],
            send_sem=moment_sems.at[0],
            recv_sem=moment_sems.at[1],
            device_id=other(step),
            device_id_type=MESH,
        ).start()
        return carry

    lax.fori_loop(1, count, share, 0)

    def around(number):
        offset = (number // 9 - 1, number // 3 % 3 - 1, number % 3 - 1)
        there = tuple(a + b for a, b in zip(here, offset))
        inside = functools.reduce(
            jnp.logical_and, [(a >= 0) & (a < size) for a, size in zip(there, sizes)]
        )
        return there, inside

    def copy(number, there):
        return pltpu.make_async_remote_copy(
            src_ref=sent_ref,
            dst_ref=near_ref.at[26 - number],
            send_sem=send_sems.at[number],
            recv_sem=recv_sems.at[26 - number],
            device_id=there,
            device_id_type=MESH,
        )

    for number in range(27):
        if number != 13:
            there, inside = around(number)

            @pl.when(inside)
            def _():
                copy(number, there).start()

    own.wait()
    rest = every_ref.at[pl.ds(1, count - 1)]
    pltpu.make_async_copy(rest, rest, moment_sems.at[0]).wait()
    pltpu.make_async_copy(rest, rest, moment_sems.at[1]).wait()
    for number in range(27):
        if number != 13:
            there, inside = around(number)

            @pl.when(inside)
            def _():
                pltpu.make_async_copy(sent_ref, sent_ref, send_sems.at[number]).wait()
                pltpu.make_async_copy(near_ref.at[number], near_ref.at[number], recv_sems.at[number]).wait()


def forces(position, velocity, mass):
    norm = jnp.sum(position * position, axis=0, keepdims=True) + 0.5 * SOFTENING
    mixed = jnp.sum(position * velocity, axis=0, keepdims=True)
    one = jnp.ones_like(norm)
    nought = jnp.zeros_like(norm)
    nought3 = jnp.zeros_like(position)
    left = jnp.concatenate([position, velocity, norm, mixed], axis=0)
    left_h, left_m, left_l = three(left)
    ones8 = jnp.ones_like(left)
    zeros8 = jnp.zeros_like(left)
    left_all = jnp.concatenate([left_h, left_h, left_h, left_m, left_m, left_l, ones8, zeros8], axis=0)

    pos_parts = three(position)
    vel_parts = three(velocity)
    norm_parts = three(norm)
    mixed_parts = three(mixed)

    def right(kind):
        if kind == 0:
            groups = [
                jnp.concatenate([-2.0 * part, nought3, one if k == 0 else nought, nought], axis=0)
                for k, part in enumerate(pos_parts)
            ]
            last = jnp.concatenate([*norm_parts, nought3, nought, nought], axis=0)
        else:
            groups = [
                jnp.concatenate([-v, -p, nought, one if k == 0 else nought], axis=0)
                for k, (p, v) in enumerate(zip(pos_parts, vel_parts))
            ]
            last = jnp.concatenate([*mixed_parts, nought3, nought, nought], axis=0)
        first, second, third = groups
        return jnp.concatenate([first, second, third, first, second, first, last, zeros8], axis=0)

    right_all = jnp.concatenate([right(0), right(1)], axis=1)
    pairs = lax.dot_general(
        left_all.astype(BF16),
        right_all.astype(BF16),
        (((0,), (0,)), ((), ())),
        preferred_element_type=F32,
    )
    square, rate = pairs[:, 0:LANES], pairs[:, LANES:]
    inverse = lax.rsqrt(square)
    radius = square * inverse
    inverse2 = inverse * inverse
    near = jnp.clip(OUTER_RADIUS / SPAN - radius * (1.0 / SPAN), 0.0, 1.0)
    weight = (near * near) * (3.0 - 2.0 * near) * (inverse * inverse2)
    turned = weight * (rate * inverse2)
    weight_h = weight.astype(BF16)
    weight_l = (weight - weight_h.astype(F32)).astype(BF16)
    turned_h = turned.astype(BF16)
    turned_l = (turned - turned_h.astype(F32)).astype(BF16)
    matrix = jnp.concatenate(
        [
            jnp.concatenate([weight_h, turned_h], axis=1),
            jnp.concatenate([weight_l, turned_l], axis=1),
        ],
        axis=0,
    )
    values = jnp.concatenate([position, velocity, one, nought], axis=0) * mass
    values = jnp.concatenate([*three(values), zeros8], axis=0).astype(BF16)
    sums = jnp.dot(jnp.concatenate([values, values], axis=1), matrix, preferred_element_type=F32)
    sums = sums[0:8] + sums[8:16] + sums[16:24]
    plain, bent = sums[:, 0:LANES], sums[:, LANES:]
    acceleration = plain[0:3] - position * plain[6:7]
    jerk = plain[3:6] - velocity * plain[6:7] - 3.0 * (bent[0:3] - position * bent[6:7])
    return acceleration, jerk


def far_field(pos_ref, every_ref, far_ref):
    stars = pos_ref.shape[1]
    domains = every_ref.shape[0]
    group = min(32, domains)

    def chunk(number, carry):
        columns = pl.ds(pl.multiple_of(number * LANES, LANES), LANES)
        star = [jnp.broadcast_to(pos_ref[axis : axis + 1, columns], (CELLS, LANES)) for axis in range(3)]

        def some(step, total):
            rows = every_ref[pl.ds(pl.multiple_of(step * group, group), group), :]
            table = rows.T
            for k in range(group):
                mass, *centre = [
                    jnp.broadcast_to(table[c * CELLS : (c + 1) * CELLS, k : k + 1], (CELLS, LANES))
                    for c in range(4)
                ]
                offset = [c - s for c, s in zip(centre, star)]
                square = offset[0] * offset[0] + offset[1] * offset[1] + offset[2] * offset[2] + SOFTENING
                inverse = lax.rsqrt(square)
                fraction = jnp.clip(square * inverse * (1.0 / SPAN) - INNER_RADIUS / SPAN, 0.0, 1.0)
                weight = mass * (fraction * fraction * (3.0 - 2.0 * fraction)) * (inverse * inverse * inverse)
                total = tuple(t + weight * o for t, o in zip(total, offset))
            return total

        total = lax.fori_loop(
            0, domains // group, some, tuple(jnp.zeros((CELLS, LANES), F32) for _ in range(3))
        )
        far_ref[:, columns] = jnp.concatenate([jnp.sum(t, axis=0, keepdims=True) for t in total], axis=0)
        return carry

    lax.fori_loop(0, stars // LANES, chunk, 0)


TOGETHER = 2


def step_stars(
    capacity, lanes, steps_ref, owner_ref, pos_ref, rows_ref, near_ref, every_ref, index_ref,
    far_ref, out_ref, member_ref, slot_ref, order_ref, tally_ref,
):
    blocks, length = index_ref.shape
    far_field(pos_ref, every_ref, far_ref)
    out_ref[...] = jnp.zeros_like(out_ref)

    def clear(i, carry):
        tally_ref[i] = 0
        return carry

    lax.fori_loop(0, tally_ref.shape[0], clear, 0)
    base = SUBMAX + 2

    def count(b, carry):
        n = steps_ref[b]
        tally_ref[n + 1] = tally_ref[n + 1] + 1
        owner = owner_ref[b, 0]
        rank = tally_ref[base + owner]
        tally_ref[base + owner] = rank + 1
        slot_ref[b] = owner * capacity + rank
        return carry

    lax.fori_loop(0, blocks, count, 0)

    def sum_up(i, carry):
        tally_ref[i] = tally_ref[i] + tally_ref[i - 1]
        return carry

    lax.fori_loop(1, base, sum_up, 0)

    def place(b, carry):
        n = steps_ref[b]
        at = tally_ref[n]
        order_ref[at] = b
        tally_ref[n] = at + 1
        return carry

    lax.fori_loop(0, blocks, place, 0)

    own_chunks = rows_ref.shape[0]
    per = near_ref.shape[1]
    group = 8
    for first in range(0, blocks, group):
        indices = [jnp.broadcast_to(index_ref[b : b + 1, :], (8, LANES)) for b in range(first, first + group)]
        lane = [i & (LANES - 1) for i in indices]
        chunk = [i >> 7 for i in indices]

        def found(piece, number, carry):
            return tuple(
                jnp.where(c == number, jnp.take_along_axis(piece, l, axis=1), old)
                for c, l, old in zip(chunk, lane, carry)
            )

        carry = tuple(jnp.zeros((8, LANES), F32) for _ in range(group))
        for number in range(own_chunks):
            carry = found(rows_ref[number], number, carry)

        def around(number, carry):
            for part in range(per):
                carry = found(near_ref[number, part], own_chunks + number * per + part, carry)
            return carry

        carry = lax.fori_loop(0, near_ref.shape[0], around, carry)
        for b, value in enumerate(carry):
            member_ref[first + b] = value

    def bunch(number, carry):
        names = [order_ref[number * TOGETHER + g] for g in range(TOGETHER)]
        counts = [steps_ref[name] for name in names]
        most = counts[-1]
        data = []
        state = []
        for name, n in zip(names, counts):
            value = member_ref[name]
            middle = jnp.sum(value[0:6], axis=1, keepdims=True) * (1.0 / length)
            moved = value[0:6] - middle
            mass = value[6:7]
            steps = jnp.full((3, LANES), n, jnp.int32)
            width = TIME_STEP / jnp.maximum(steps.astype(F32), 1.0)
            drift = jnp.broadcast_to(middle[3:6], (3, LANES)) * TIME_STEP
            data.append((mass, steps, width, drift, moved))
            position, velocity = moved[0:3], moved[3:6]
            state.append((position, velocity, *forces(position, velocity, mass)))

        def advance(step, state):
            after = []
            for (mass, steps, width, drift, moved), (position, velocity, acc, jerk) in zip(data, state):
                squared = width * width
                predicted = (
                    position + width * velocity + 0.5 * squared * acc + squared * width * (1.0 / 6.0) * jerk
                )
                predicted_vel = velocity + width * acc + 0.5 * squared * jerk
                acc_new, jerk_new = forces(predicted, predicted_vel, mass)
                velocity_new = (
                    velocity + 0.5 * width * (acc + acc_new) + squared * (1.0 / 12.0) * (jerk - jerk_new)
                )
                position_new = (
                    position + 0.5 * width * (velocity + velocity_new) + squared * (1.0 / 12.0) * (acc - acc_new)
                )
                live = steps > step
                after.append(
                    tuple(
                        jnp.where(live, new, old)
                        for new, old in (
                            (position_new, position), (velocity_new, velocity), (acc_new, acc), (jerk_new, jerk),
                        )
                    )
                )
            return tuple(after)

        state = lax.fori_loop(0, most, advance, tuple(state))
        for name, (mass, steps, width, drift, moved), (position, velocity, acc, jerk) in zip(names, data, state):
            change = jnp.concatenate([position - moved[0:3] + drift, velocity - moved[3:6]], axis=0)
            at = pl.multiple_of(slot_ref[name] * length, length)
            out_ref[:, pl.ds(at, length)] = change
        return carry

    lax.fori_loop(0, blocks // TOGETHER, bunch, 0)


def deliver(lanes, packed_ref, out_ref, own_sem, sems):
    here = tuple(lax.axis_index(axis) for axis in AXES)
    me = here[2]
    part = packed_ref.shape[1] // lanes
    barrier = pltpu.get_barrier_semaphore()

    def columns(number):
        return pl.ds(pl.multiple_of(number * part, LANES), part)

    own = pltpu.make_async_copy(packed_ref.at[:, columns(me)], out_ref.at[:, columns(me)], own_sem)
    own.start()

    def other(step):
        there = lax.rem(me + step, lanes)
        return there, (here[0], here[1], there)

    def greet(step, carry):
        pl.semaphore_signal(barrier, inc=1, device_id=other(step)[1], device_id_type=MESH)
        return carry

    lax.fori_loop(1, lanes, greet, 0)
    pl.semaphore_wait(barrier, lanes - 1)

    def send(step, carry):
        there, device = other(step)
        pltpu.make_async_remote_copy(
            src_ref=packed_ref.at[:, columns(there)],
            dst_ref=out_ref.at[:, columns(me)],
            send_sem=sems.at[0],
            recv_sem=sems.at[1],
            device_id=device,
            device_id_type=MESH,
        ).start()
        return carry

    lax.fori_loop(1, lanes, send, 0)
    own.wait()
    rest = packed_ref.at[:, pl.ds(0, (lanes - 1) * part)]
    pltpu.make_async_copy(rest, rest, sems.at[0]).wait()
    pltpu.make_async_copy(rest, rest, sems.at[1]).wait()


def vmem(count):
    return [pl.BlockSpec(memory_space=pltpu.VMEM)] * count


def on_device(
    sizes, positions, velocities, star_mass, far_previous, cell_index, ghost_list, block_index, block_owner, substeps
):
    lanes = sizes[2]
    domains = sizes[0] * sizes[1] * sizes[2]
    blocks, length = block_index.shape
    capacity = max(2, 2 * BLOCKS_DEV // lanes)
    stars, ghosts = positions.shape[1], ghost_list.shape[0]
    shape = jax.ShapeDtypeStruct
    rows, sent, moment = pl.pallas_call(
        prepare,
        out_shape=(
            shape((stars // LANES, 8, LANES), F32),
            shape((ghosts // LANES, 8, LANES), F32),
            shape((1, 1, LANES), F32),
        ),
        in_specs=vmem(6),
        out_specs=tuple(vmem(3)),
        name="prepare",
    )(
        positions,
        velocities,
        star_mass.reshape(1, stars),
        far_previous,
        cell_index.reshape(1, stars),
        ghost_list.reshape(1, ghosts),
    )
    near, every = pl.pallas_call(
        functools.partial(exchange, sizes),
        out_shape=(shape((27, *sent.shape), F32), shape((domains, 1, LANES), F32)),
        in_specs=vmem(2),
        out_specs=tuple(vmem(2)),
        scratch_shapes=[
            pltpu.SemaphoreType.DMA,
            pltpu.SemaphoreType.DMA((2,)),
            pltpu.SemaphoreType.DMA((27,)),
            pltpu.SemaphoreType.DMA((27,)),
        ],
        compiler_params=pltpu.CompilerParams(collective_id=0, has_side_effects=True),
        name="exchange",
    )(sent, moment)
    smem = pl.BlockSpec(memory_space=pltpu.SMEM)
    far_acc, packed = pl.pallas_call(
        functools.partial(step_stars, capacity, lanes),
        out_shape=(shape((3, stars), F32), shape((6, lanes * capacity * length), F32)),
        in_specs=[smem, smem, *vmem(5)],
        out_specs=tuple(vmem(2)),
        scratch_shapes=[
            pltpu.VMEM((blocks, 8, LANES), F32),
            pltpu.SMEM((blocks,), jnp.int32),
            pltpu.SMEM((blocks,), jnp.int32),
            pltpu.SMEM((SUBMAX + 2 + lanes,), jnp.int32),
        ],
        name="step_stars",
    )(substeps, block_owner, positions, rows, near, every.reshape(domains, LANES), block_index)
    arrived = pl.pallas_call(
        functools.partial(deliver, lanes),
        out_shape=shape(packed.shape, F32),
        in_specs=vmem(1),
        out_specs=vmem(1)[0],
        scratch_shapes=[pltpu.SemaphoreType.DMA, pltpu.SemaphoreType.DMA((2,))],
        compiler_params=pltpu.CompilerParams(collective_id=1, has_side_effects=True),
        name="deliver",
    )(packed)
    return far_acc, arrived


def solution(mesh):
    split = P(AXES)
    wide = P(None, AXES)
    tall = P(AXES, None)
    return jax.shard_map(
        functools.partial(on_device, tuple(mesh.shape[axis] for axis in AXES)),
        mesh=mesh,
        in_specs=(wide, wide, split, wide, split, split, tall, tall, split),
        out_specs=(wide, wide),
        check_vma=False,
    )
```

```python
import functools

import jax
import jax.numpy as jnp
from jax import lax
from jax.experimental import pallas as pl
from jax.experimental.pallas import tpu as pltpu
from jax.sharding import PartitionSpec as P

CELLS = 16
BLOCKS_DEV = 16
SUBMAX = 8
AXES = ("gx", "gy", "gz")
MESH = pl.DeviceIdType.MESH
LANES = 128

SOFTENING = 0.0025
INNER_RADIUS = 0.25
OUTER_RADIUS = 1.0
TIME_STEP = 0.25
SPAN = OUTER_RADIUS - INNER_RADIUS

BF16 = jnp.bfloat16
F32 = jnp.float32


def three(value):
    high = value.astype(BF16).astype(F32)
    rest = value - high
    middle = rest.astype(BF16).astype(F32)
    low = (rest - middle).astype(BF16).astype(F32)
    return high, middle, low


def pick(chunks, index):
    index = jnp.broadcast_to(index, (8, LANES))
    lane, chunk = index & (LANES - 1), index >> 7
    found = jnp.zeros((8, LANES), F32)
    for number, piece in chunks:
        found = jnp.where(chunk == number, jnp.take_along_axis(piece, lane, axis=1), found)
    return found


def prepare(pos_ref, vel_ref, mass_ref, far_ref, cell_ref, ghost_ref, rows_ref, sent_ref, moment_ref):
    stars = pos_ref.shape[1]
    position, mass = pos_ref[...], mass_ref[...]
    kicked = vel_ref[...] + far_ref[...] * (0.5 * TIME_STEP)
    rows = jnp.concatenate([position, kicked, mass, jnp.zeros((1, stars), F32)], axis=0)
    chunks = []
    for number in range(stars // LANES):
        piece = rows[:, number * LANES : (number + 1) * LANES]
        rows_ref[number] = piece
        chunks.append((number, piece))
    for number in range(ghost_ref.shape[1] // LANES):
        sent_ref[number] = pick(chunks, ghost_ref[:, number * LANES : (number + 1) * LANES])
    cell = lax.broadcasted_iota(jnp.int32, (LANES, stars), 0)
    member = jnp.where(jnp.broadcast_to(cell_ref[...], (LANES, stars)) == cell, 1.0, 0.0).astype(BF16)
    weighted = jnp.concatenate([mass, position * mass, jnp.zeros((4, stars), F32)], axis=0)
    parts = jnp.concatenate([*three(weighted), jnp.zeros_like(weighted)], axis=0).astype(BF16)
    sums = lax.dot_general(parts, member, (((1,), (1,)), ((), ())), preferred_element_type=F32)
    sums = sums[0:8] + sums[8:16] + sums[16:24]
    inside = lax.broadcasted_iota(jnp.int32, (1, LANES), 1) < CELLS
    total = jnp.where(inside, sums[0:1], 0.0)
    packed = total
    for axis in range(3):
        centre = jnp.where(inside, sums[axis + 1 : axis + 2] / jnp.where(inside, total, 1.0), 0.0)
        packed = packed + pltpu.roll(centre, (axis + 1) * CELLS, 1)
    moment_ref[0] = packed


def coordinates(sizes, number):
    return number // (sizes[1] * sizes[2]), number // sizes[2] % sizes[1], number % sizes[2]


def exchange(sizes, sent_ref, moment_ref, near_ref, every_ref, own_sem, moment_sems, send_sems, recv_sems):
    count = sizes[0] * sizes[1] * sizes[2]
    here = tuple(lax.axis_index(axis) for axis in AXES)
    me = (here[0] * sizes[1] + here[1]) * sizes[2] + here[2]
    barrier = pltpu.get_barrier_semaphore()

    def other(step):
        return coordinates(sizes, lax.rem(me + step, count))

    def greet(step, carry):
        pl.semaphore_signal(barrier, inc=1, device_id=other(step), device_id_type=MESH)
        return carry

    lax.fori_loop(1, count, greet, 0)
    own = pltpu.make_async_copy(moment_ref.at[0], every_ref.at[0], own_sem)
    own.start()
    pl.semaphore_wait(barrier, count - 1)

    def share(step, carry):
        pltpu.make_async_remote_copy(
            src_ref=moment_ref.at[0],
            dst_ref=every_ref.at[step],
            send_sem=moment_sems.at[0],
            recv_sem=moment_sems.at[1],
            device_id=other(step),
            device_id_type=MESH,
        ).start()
        return carry

    lax.fori_loop(1, count, share, 0)

    def around(number):
        offset = (number // 9 - 1, number // 3 % 3 - 1, number % 3 - 1)
        there = tuple(a + b for a, b in zip(here, offset))
        inside = functools.reduce(
            jnp.logical_and, [(a >= 0) & (a < size) for a, size in zip(there, sizes)]
        )
        return there, inside

    def copy(number, there):
        return pltpu.make_async_remote_copy(
            src_ref=sent_ref,
            dst_ref=near_ref.at[26 - number],
            send_sem=send_sems.at[number],
            recv_sem=recv_sems.at[26 - number],
            device_id=there,
            device_id_type=MESH,
        )

    for number in range(27):
        if number != 13:
            there, inside = around(number)

            @pl.when(inside)
            def _():
                copy(number, there).start()

    own.wait()
    rest = every_ref.at[pl.ds(1, count - 1)]
    pltpu.make_async_copy(rest, rest, moment_sems.at[0]).wait()
    pltpu.make_async_copy(rest, rest, moment_sems.at[1]).wait()
    for number in range(27):
        if number != 13:
            there, inside = around(number)

            @pl.when(inside)
            def _():
                pltpu.make_async_copy(sent_ref, sent_ref, send_sems.at[number]).wait()
                pltpu.make_async_copy(near_ref.at[number], near_ref.at[number], recv_sems.at[number]).wait()


def forces(position, velocity, mass):
    norm = jnp.sum(position * position, axis=0, keepdims=True) + 0.5 * SOFTENING
    mixed = jnp.sum(position * velocity, axis=0, keepdims=True)
    one = jnp.ones_like(norm)
    nought = jnp.zeros_like(norm)
    nought3 = jnp.zeros_like(position)
    left = jnp.concatenate([position, velocity, norm, mixed], axis=0)
    left_h, left_m, left_l = three(left)
    ones8 = jnp.ones_like(left)
    zeros8 = jnp.zeros_like(left)
    left_all = jnp.concatenate([left_h, left_h, left_h, left_m, left_m, left_l, ones8, zeros8], axis=0)

    pos_parts = three(position)
    vel_parts = three(velocity)
    norm_parts = three(norm)
    mixed_parts = three(mixed)

    def right(kind):
        if kind == 0:
            groups = [
                jnp.concatenate([-2.0 * part, nought3, one if k == 0 else nought, nought], axis=0)
                for k, part in enumerate(pos_parts)
            ]
            last = jnp.concatenate([*norm_parts, nought3, nought, nought], axis=0)
        else:
            groups = [
                jnp.concatenate([-v, -p, nought, one if k == 0 else nought], axis=0)
                for k, (p, v) in enumerate(zip(pos_parts, vel_parts))
            ]
            last = jnp.concatenate([*mixed_parts, nought3, nought, nought], axis=0)
        first, second, third = groups
        return jnp.concatenate([first, second, third, first, second, first, last, zeros8], axis=0)

    right_all = jnp.concatenate([right(0), right(1)], axis=1)
    pairs = lax.dot_general(
        left_all.astype(BF16),
        right_all.astype(BF16),
        (((0,), (0,)), ((), ())),
        preferred_element_type=F32,
    )
    square, rate = pairs[:, 0:LANES], pairs[:, LANES:]
    inverse = lax.rsqrt(square)
    radius = square * inverse
    inverse2 = inverse * inverse
    near = jnp.clip(OUTER_RADIUS / SPAN - radius * (1.0 / SPAN), 0.0, 1.0)
    weight = (near * near) * (3.0 - 2.0 * near) * (inverse * inverse2)
    turned = weight * (rate * inverse2)
    weight_h = weight.astype(BF16)
    weight_l = (weight - weight_h.astype(F32)).astype(BF16)
    turned_h = turned.astype(BF16)
    turned_l = (turned - turned_h.astype(F32)).astype(BF16)
    matrix = jnp.concatenate(
        [
            jnp.concatenate([weight_h, turned_h], axis=1),
            jnp.concatenate([weight_l, turned_l], axis=1),
        ],
        axis=0,
    )
    values = jnp.concatenate([position, velocity, one, nought], axis=0) * mass
    values = jnp.concatenate([*three(values), zeros8], axis=0).astype(BF16)
    sums = jnp.dot(jnp.concatenate([values, values], axis=1), matrix, preferred_element_type=F32)
    sums = sums[0:8] + sums[8:16] + sums[16:24]
    plain, bent = sums[:, 0:LANES], sums[:, LANES:]
    acceleration = plain[0:3] - position * plain[6:7]
    jerk = plain[3:6] - velocity * plain[6:7] - 3.0 * (bent[0:3] - position * bent[6:7])
    return acceleration, jerk


def far_field(pos_ref, every_ref, far_ref):
    stars = pos_ref.shape[1]
    domains = every_ref.shape[0]
    group = min(32, domains)

    def chunk(number, carry):
        columns = pl.ds(pl.multiple_of(number * LANES, LANES), LANES)
        star = [jnp.broadcast_to(pos_ref[axis : axis + 1, columns], (CELLS, LANES)) for axis in range(3)]

        def some(step, total):
            rows = every_ref[pl.ds(pl.multiple_of(step * group, group), group), :]
            table = rows.T
            for k in range(group):
                mass, *centre = [
                    jnp.broadcast_to(table[c * CELLS : (c + 1) * CELLS, k : k + 1], (CELLS, LANES))
                    for c in range(4)
                ]
                offset = [c - s for c, s in zip(centre, star)]
                square = offset[0] * offset[0] + offset[1] * offset[1] + offset[2] * offset[2] + SOFTENING
                inverse = lax.rsqrt(square)
                fraction = jnp.clip(square * inverse * (1.0 / SPAN) - INNER_RADIUS / SPAN, 0.0, 1.0)
                weight = mass * (fraction * fraction * (3.0 - 2.0 * fraction)) * (inverse * inverse * inverse)
                total = tuple(t + weight * o for t, o in zip(total, offset))
            return total

        total = lax.fori_loop(
            0, domains // group, some, tuple(jnp.zeros((CELLS, LANES), F32) for _ in range(3))
        )
        far_ref[:, columns] = jnp.concatenate([jnp.sum(t, axis=0, keepdims=True) for t in total], axis=0)
        return carry

    lax.fori_loop(0, stars // LANES, chunk, 0)


TOGETHER = 8


def step_stars(
    sizes, capacity, steps_ref, owner_ref, rows_ref, near_ref, index_ref, out_ref, member_ref, slot_ref, order_ref,
):
    blocks, length = index_ref.shape
    out_ref[...] = jnp.zeros_like(out_ref)

    counts = [steps_ref[b] for b in range(blocks)]
    owners = [owner_ref[b] for b in range(blocks)]
    places = [jnp.int32(0)] * blocks
    for b in range(blocks):
        rank = jnp.int32(0)
        for earlier in range(b):
            before = (counts[earlier] <= counts[b]).astype(jnp.int32)
            places[b] = places[b] + before
            places[earlier] = places[earlier] + (1 - before)
            rank = rank + (owners[earlier] == owners[b]).astype(jnp.int32)
        slot_ref[b] = owners[b] * capacity + rank
    for b in range(blocks):
        order_ref[places[b]] = b

    own_chunks = rows_ref.shape[0]
    per = near_ref.shape[1]
    indices = [jnp.broadcast_to(index_ref[b : b + 1, :], (8, LANES)) for b in range(blocks)]
    lane = [i & (LANES - 1) for i in indices]
    chunk = [i >> 7 for i in indices]

    def found(piece, number, carry):
        return tuple(
            jnp.where(c == number, jnp.take_along_axis(piece, l, axis=1), old)
            for c, l, old in zip(chunk, lane, carry)
        )

    carry = tuple(jnp.zeros((8, LANES), F32) for _ in range(blocks))
    for number in range(own_chunks):
        carry = found(rows_ref[number], number, carry)
    def reach(slot, carry):
        for part in range(per):
            carry = found(near_ref[slot, part], own_chunks + slot * per + part, carry)
        return carry

    bounds = []
    for axis, size in zip(AXES, sizes):
        at = lax.axis_index(axis)
        bounds.append((jnp.where(at > 0, 0, 1), jnp.where(at < size - 1, 3, 2)))
    (low_x, high_x), (low_y, high_y), (low_z, high_z) = bounds
    wide_y, wide_z = high_y - low_y, high_z - low_z

    def visit(step, carry):
        number = (low_x + step // (wide_y * wide_z)) * 9
        number = number + (low_y + step // wide_z % wide_y) * 3 + low_z + step % wide_z
        return reach(number, carry)

    carry = lax.fori_loop(0, (high_x - low_x) * wide_y * wide_z, visit, carry)
    for b, value in enumerate(carry):
        member_ref[b] = value

    def bunch(number, carry):
        names = [order_ref[number * TOGETHER + g] for g in range(TOGETHER)]
        counts = [steps_ref[name] for name in names]
        most = counts[-1]
        data = []
        state = []
        for name, n in zip(names, counts):
            value = member_ref[name]
            middle = jnp.sum(value[0:6], axis=1, keepdims=True) * (1.0 / length)
            moved = value[0:6] - middle
            mass = value[6:7]
            steps = jnp.full((3, LANES), n, jnp.int32)
            width = TIME_STEP / jnp.maximum(steps.astype(F32), 1.0)
            drift = jnp.broadcast_to(middle[3:6], (3, LANES)) * TIME_STEP
            data.append((mass, steps, width, drift, moved))
            position, velocity = moved[0:3], moved[3:6]
            state.append((position, velocity, *forces(position, velocity, mass)))

        def advance(step, state):
            after = []
            for (mass, steps, width, drift, moved), (position, velocity, acc, jerk) in zip(data, state):
                squared = width * width
                predicted = (
                    position + width * velocity + 0.5 * squared * acc + squared * width * (1.0 / 6.0) * jerk
                )
                predicted_vel = velocity + width * acc + 0.5 * squared * jerk
                acc_new, jerk_new = forces(predicted, predicted_vel, mass)
                velocity_new = (
                    velocity + 0.5 * width * (acc + acc_new) + squared * (1.0 / 12.0) * (jerk - jerk_new)
                )
                position_new = (
                    position + 0.5 * width * (velocity + velocity_new) + squared * (1.0 / 12.0) * (acc - acc_new)
                )
                live = steps > step
                after.append(
                    tuple(
                        jnp.where(live, new, old)
                        for new, old in (
                            (position_new, position), (velocity_new, velocity), (acc_new, acc), (jerk_new, jerk),
                        )
                    )
                )
            return tuple(after)

        state = lax.fori_loop(0, most, advance, tuple(state))
        for name, (mass, steps, width, drift, moved), (position, velocity, acc, jerk) in zip(names, data, state):
            change = jnp.concatenate([position - moved[0:3] + drift, velocity - moved[3:6]], axis=0)
            at = pl.multiple_of(slot_ref[name] * length, length)
            out_ref[:, pl.ds(at, length)] = change
        return carry

    lax.fori_loop(0, blocks // TOGETHER, bunch, 0)


def deliver(lanes, packed_ref, pos_ref, every_ref, out_ref, far_ref, own_sem, sems):
    here = tuple(lax.axis_index(axis) for axis in AXES)
    me = here[2]
    part = packed_ref.shape[1] // lanes
    barrier = pltpu.get_barrier_semaphore()

    def columns(number):
        return pl.ds(pl.multiple_of(number * part, LANES), part)

    own = pltpu.make_async_copy(packed_ref.at[:, columns(me)], out_ref.at[:, columns(me)], own_sem)
    own.start()

    def other(step):
        there = lax.rem(me + step, lanes)
        return there, (here[0], here[1], there)

    def greet(step, carry):
        pl.semaphore_signal(barrier, inc=1, device_id=other(step)[1], device_id_type=MESH)
        return carry

    lax.fori_loop(1, lanes, greet, 0)
    pl.semaphore_wait(barrier, lanes - 1)

    def send(step, carry):
        there, device = other(step)
        pltpu.make_async_remote_copy(
            src_ref=packed_ref.at[:, columns(there)],
            dst_ref=out_ref.at[:, columns(me)],
            send_sem=sems.at[0],
            recv_sem=sems.at[1],
            device_id=device,
            device_id_type=MESH,
        ).start()
        return carry

    lax.fori_loop(1, lanes, send, 0)
    far_field(pos_ref, every_ref, far_ref)
    own.wait()
    rest = packed_ref.at[:, pl.ds(0, (lanes - 1) * part)]
    pltpu.make_async_copy(rest, rest, sems.at[0]).wait()
    pltpu.make_async_copy(rest, rest, sems.at[1]).wait()


def vmem(count):
    return [pl.BlockSpec(memory_space=pltpu.VMEM)] * count


def on_device(
    sizes, positions, velocities, star_mass, far_previous, cell_index, ghost_list, block_index, block_owner, substeps
):
    lanes = sizes[2]
    domains = sizes[0] * sizes[1] * sizes[2]
    blocks, length = block_index.shape
    capacity = max(2, 2 * BLOCKS_DEV // lanes)
    stars, ghosts = positions.shape[1], ghost_list.shape[0]
    shape = jax.ShapeDtypeStruct
    rows, sent, moment = pl.pallas_call(
        prepare,
        out_shape=(
            shape((stars // LANES, 8, LANES), F32),
            shape((ghosts // LANES, 8, LANES), F32),
            shape((1, 1, LANES), F32),
        ),
        in_specs=vmem(6),
        out_specs=tuple(vmem(3)),
        name="prepare",
    )(
        positions,
        velocities,
        star_mass.reshape(1, stars),
        far_previous,
        cell_index.reshape(1, stars),
        ghost_list.reshape(1, ghosts),
    )
    near, every = pl.pallas_call(
        functools.partial(exchange, sizes),
        out_shape=(shape((27, *sent.shape), F32), shape((domains, 1, LANES), F32)),
        in_specs=vmem(2),
        out_specs=tuple(vmem(2)),
        scratch_shapes=[
            pltpu.SemaphoreType.DMA,
            pltpu.SemaphoreType.DMA((2,)),
            pltpu.SemaphoreType.DMA((27,)),
            pltpu.SemaphoreType.DMA((27,)),
        ],
        compiler_params=pltpu.CompilerParams(collective_id=0, has_side_effects=True),
        name="exchange",
    )(sent, moment)
    smem = pl.BlockSpec(memory_space=pltpu.SMEM)
    packed = pl.pallas_call(
        functools.partial(step_stars, sizes, capacity),
        out_shape=shape((6, lanes * capacity * length), F32),
        in_specs=[smem, smem, *vmem(3)],
        out_specs=vmem(1)[0],
        scratch_shapes=[
            pltpu.VMEM((blocks, 8, LANES), F32),
            pltpu.SMEM((blocks,), jnp.int32),
            pltpu.SMEM((blocks,), jnp.int32),
        ],
        name="step_stars",
    )(substeps, block_owner.reshape(blocks), rows, near, block_index)
    arrived, far_acc = pl.pallas_call(
        functools.partial(deliver, lanes),
        out_shape=(shape(packed.shape, F32), shape((3, stars), F32)),
        in_specs=vmem(3),
        out_specs=tuple(vmem(2)),
        scratch_shapes=[pltpu.SemaphoreType.DMA, pltpu.SemaphoreType.DMA((2,))],
        compiler_params=pltpu.CompilerParams(collective_id=1, has_side_effects=True),
        name="deliver",
    )(packed, positions, every.reshape(domains, LANES))
    return far_acc, arrived


def solution(mesh):
    split = P(AXES)
    wide = P(None, AXES)
    tall = P(AXES, None)
    return jax.shard_map(
        functools.partial(on_device, tuple(mesh.shape[axis] for axis in AXES)),
        mesh=mesh,
        in_specs=(wide, wide, split, wide, split, split, tall, tall, split),
        out_specs=(wide, wide),
        check_vma=False,
    )
```

```python
import functools

import jax
import jax.numpy as jnp
from jax import lax
from jax.experimental import pallas as pl
from jax.experimental.pallas import tpu as pltpu
from jax.sharding import PartitionSpec as P

CELLS = 16
BLOCKS_DEV = 16
SUBMAX = 8
AXES = ("gx", "gy", "gz")
MESH = pl.DeviceIdType.MESH
LANES = 128

SOFTENING = 0.0025
INNER_RADIUS = 0.25
OUTER_RADIUS = 1.0
TIME_STEP = 0.25
SPAN = OUTER_RADIUS - INNER_RADIUS

BF16 = jnp.bfloat16
F32 = jnp.float32


def three(value):
    high = value.astype(BF16).astype(F32)
    rest = value - high
    middle = rest.astype(BF16).astype(F32)
    low = (rest - middle).astype(BF16).astype(F32)
    return high, middle, low


def pick(chunks, index):
    index = jnp.broadcast_to(index, (8, LANES))
    lane, chunk = index & (LANES - 1), index >> 7
    found = jnp.zeros((8, LANES), F32)
    for number, piece in chunks:
        found = jnp.where(chunk == number, jnp.take_along_axis(piece, lane, axis=1), found)
    return found


def prepare(pos_ref, vel_ref, mass_ref, far_ref, cell_ref, ghost_ref, rows_ref, sent_ref, moment_ref):
    stars = pos_ref.shape[1]
    position, mass = pos_ref[...], mass_ref[...]
    kicked = vel_ref[...] + far_ref[...] * (0.5 * TIME_STEP)
    rows = jnp.concatenate([position, kicked, mass, jnp.zeros((1, stars), F32)], axis=0)
    chunks = []
    for number in range(stars // LANES):
        piece = rows[:, number * LANES : (number + 1) * LANES]
        rows_ref[number] = piece
        chunks.append((number, piece))
    for number in range(ghost_ref.shape[1] // LANES):
        sent_ref[number] = pick(chunks, ghost_ref[:, number * LANES : (number + 1) * LANES])
    cell = lax.broadcasted_iota(jnp.int32, (LANES, stars), 0)
    member = jnp.where(jnp.broadcast_to(cell_ref[...], (LANES, stars)) == cell, 1.0, 0.0).astype(BF16)
    weighted = jnp.concatenate([mass, position * mass, jnp.zeros((4, stars), F32)], axis=0)
    parts = jnp.concatenate([*three(weighted), jnp.zeros_like(weighted)], axis=0).astype(BF16)
    sums = lax.dot_general(parts, member, (((1,), (1,)), ((), ())), preferred_element_type=F32)
    sums = sums[0:8] + sums[8:16] + sums[16:24]
    inside = lax.broadcasted_iota(jnp.int32, (1, LANES), 1) < CELLS
    total = jnp.where(inside, sums[0:1], 0.0)
    packed = total
    for axis in range(3):
        centre = jnp.where(inside, sums[axis + 1 : axis + 2] / jnp.where(inside, total, 1.0), 0.0)
        packed = packed + pltpu.roll(centre, (axis + 1) * CELLS, 1)
    moment_ref[0] = packed


def coordinates(sizes, number):
    return number // (sizes[1] * sizes[2]), number // sizes[2] % sizes[1], number % sizes[2]


def exchange(
    sizes, pos_ref, vel_ref, mass_ref, far_ref, cell_ref, ghost_ref, rows_ref, near_ref, every_ref,
    sent_ref, moment_ref, own_sem, moment_sems, send_sems, recv_sems,
):
    count = sizes[0] * sizes[1] * sizes[2]
    here = tuple(lax.axis_index(axis) for axis in AXES)
    me = (here[0] * sizes[1] + here[1]) * sizes[2] + here[2]
    barrier = pltpu.get_barrier_semaphore()

    def other(step):
        return coordinates(sizes, lax.rem(me + step, count))

    def greet(step, carry):
        pl.semaphore_signal(barrier, inc=1, device_id=other(step), device_id_type=MESH)
        return carry

    lax.fori_loop(1, count, greet, 0)
    prepare(pos_ref, vel_ref, mass_ref, far_ref, cell_ref, ghost_ref, rows_ref, sent_ref, moment_ref)
    own = pltpu.make_async_copy(moment_ref.at[0], every_ref.at[0], own_sem)
    own.start()
    pl.semaphore_wait(barrier, count - 1)

    def share(step, carry):
        pltpu.make_async_remote_copy(
            src_ref=moment_ref.at[0],
            dst_ref=every_ref.at[step],
            send_sem=moment_sems.at[0],
            recv_sem=moment_sems.at[1],
            device_id=other(step),
            device_id_type=MESH,
        ).start()
        return carry

    lax.fori_loop(1, count, share, 0)

    def around(number):
        offset = (number // 9 - 1, number // 3 % 3 - 1, number % 3 - 1)
        there = tuple(a + b for a, b in zip(here, offset))
        inside = functools.reduce(
            jnp.logical_and, [(a >= 0) & (a < size) for a, size in zip(there, sizes)]
        )
        return there, inside

    def copy(number, there):
        return pltpu.make_async_remote_copy(
            src_ref=sent_ref,
            dst_ref=near_ref.at[26 - number],
            send_sem=send_sems.at[number],
            recv_sem=recv_sems.at[26 - number],
            device_id=there,
            device_id_type=MESH,
        )

    for number in range(27):
        if number != 13:
            there, inside = around(number)

            @pl.when(inside)
            def _():
                copy(number, there).start()

    own.wait()
    rest = every_ref.at[pl.ds(1, count - 1)]
    pltpu.make_async_copy(rest, rest, moment_sems.at[0]).wait()
    pltpu.make_async_copy(rest, rest, moment_sems.at[1]).wait()
    for number in range(27):
        if number != 13:
            there, inside = around(number)

            @pl.when(inside)
            def _():
                pltpu.make_async_copy(sent_ref, sent_ref, send_sems.at[number]).wait()
                pltpu.make_async_copy(near_ref.at[number], near_ref.at[number], recv_sems.at[number]).wait()


def forces(position, velocity, mass):
    norm = jnp.sum(position * position, axis=0, keepdims=True) + 0.5 * SOFTENING
    mixed = jnp.sum(position * velocity, axis=0, keepdims=True)
    nought = jnp.zeros((2, LANES), F32)
    row = lax.broadcasted_iota(jnp.int32, (8, LANES), 0)
    state_row, norm_row, mixed_row = row < 6, row == 6, row == 7
    norm_one, mixed_one = jnp.where(norm_row, 1.0, 0.0), jnp.where(mixed_row, 1.0, 0.0)
    scale = jnp.where(row < 3, -2.0, 0.0)
    left = jnp.concatenate([position, velocity, norm, mixed], axis=0)
    high, middle, low = three(left)
    high_one, middle_one = jnp.where(state_row, high, 1.0), jnp.where(state_row, middle, 1.0)
    left_all = jnp.concatenate([high, high_one, high_one, middle, middle_one, low], axis=0)
    turn = three(jnp.concatenate([-velocity, -position, nought], axis=0))

    def right(parts, mine, one):
        first = jnp.where(mine, one, parts[0])
        second = jnp.where(mine, high, parts[1])
        third = jnp.where(mine, middle, parts[2])
        fourth = jnp.where(mine, low, parts[1])
        return jnp.concatenate([first, second, third, first, fourth, first], axis=0)

    right_all = jnp.concatenate(
        [right((high * scale, middle * scale, low * scale), norm_row, norm_one), right(turn, mixed_row, mixed_one)],
        axis=1,
    )
    pairs = lax.dot_general(
        left_all.astype(BF16),
        right_all.astype(BF16),
        (((0,), (0,)), ((), ())),
        preferred_element_type=F32,
    )
    square, rate = pairs[:, 0:LANES], pairs[:, LANES:]
    inverse = lax.rsqrt(square)
    radius = square * inverse
    inverse2 = inverse * inverse
    near = jnp.clip(OUTER_RADIUS / SPAN - radius * (1.0 / SPAN), 0.0, 1.0)
    weight = (near * near) * (3.0 - 2.0 * near) * (inverse * inverse2)
    turned = weight * (rate * inverse2)
    weight_h = weight.astype(BF16)
    weight_l = (weight - weight_h.astype(F32)).astype(BF16)
    turned_h = turned.astype(BF16)
    turned_l = (turned - turned_h.astype(F32)).astype(BF16)
    matrix = jnp.concatenate(
        [
            jnp.concatenate([weight_h, turned_h], axis=1),
            jnp.concatenate([weight_l, turned_l], axis=1),
        ],
        axis=0,
    )
    values = jnp.where(state_row, left, norm_one) * mass
    values = jnp.concatenate([*three(values), jnp.zeros_like(values)], axis=0).astype(BF16)
    sums = jnp.dot(jnp.concatenate([values, values], axis=1), matrix, preferred_element_type=F32)
    sums = sums[0:8] + sums[8:16] + sums[16:24]
    plain, bent = sums[:, 0:LANES], sums[:, LANES:]
    acceleration = plain[0:3] - position * plain[6:7]
    jerk = plain[3:6] - velocity * plain[6:7] - 3.0 * (bent[0:3] - position * bent[6:7])
    return acceleration, jerk


def far_field(pos_ref, every_ref, far_ref):
    stars = pos_ref.shape[1]
    domains = every_ref.shape[0]
    group = min(32, domains)

    def chunk(number, carry):
        columns = pl.ds(pl.multiple_of(number * LANES, LANES), LANES)
        star = [jnp.broadcast_to(pos_ref[axis : axis + 1, columns], (CELLS, LANES)) for axis in range(3)]

        def some(step, total):
            rows = every_ref[pl.ds(pl.multiple_of(step * group, group), group), :]
            table = rows.T
            for k in range(group):
                mass, *centre = [
                    jnp.broadcast_to(table[c * CELLS : (c + 1) * CELLS, k : k + 1], (CELLS, LANES))
                    for c in range(4)
                ]
                offset = [c - s for c, s in zip(centre, star)]
                square = offset[0] * offset[0] + offset[1] * offset[1] + offset[2] * offset[2] + SOFTENING
                inverse = lax.rsqrt(square)
                fraction = jnp.clip(square * inverse * (1.0 / SPAN) - INNER_RADIUS / SPAN, 0.0, 1.0)
                weight = mass * (fraction * fraction * (3.0 - 2.0 * fraction)) * (inverse * inverse * inverse)
                total = tuple(t + weight * o for t, o in zip(total, offset))
            return total

        total = lax.fori_loop(
            0, domains // group, some, tuple(jnp.zeros((CELLS, LANES), F32) for _ in range(3))
        )
        far_ref[:, columns] = jnp.concatenate([jnp.sum(t, axis=0, keepdims=True) for t in total], axis=0)
        return carry

    lax.fori_loop(0, stars // LANES, chunk, 0)


TOGETHER = 8


def step_stars(
    sizes, capacity, steps_ref, owner_ref, rows_ref, near_ref, index_ref, out_ref, member_ref, slot_ref, order_ref,
):
    blocks, length = index_ref.shape
    out_ref[...] = jnp.zeros_like(out_ref)

    counts = [steps_ref[b] for b in range(blocks)]
    owners = [owner_ref[b] for b in range(blocks)]
    places = [jnp.int32(0)] * blocks
    for b in range(blocks):
        rank = jnp.int32(0)
        for earlier in range(b):
            before = (counts[earlier] <= counts[b]).astype(jnp.int32)
            places[b] = places[b] + before
            places[earlier] = places[earlier] + (1 - before)
            rank = rank + (owners[earlier] == owners[b]).astype(jnp.int32)
        slot_ref[b] = owners[b] * capacity + rank
    for b in range(blocks):
        order_ref[places[b]] = b

    own_chunks = rows_ref.shape[0]
    per = near_ref.shape[1]
    indices = [jnp.broadcast_to(index_ref[b : b + 1, :], (8, LANES)) for b in range(blocks)]
    lane = [i & (LANES - 1) for i in indices]
    chunk = [i >> 7 for i in indices]

    def found(piece, number, carry):
        return tuple(
            jnp.where(c == number, jnp.take_along_axis(piece, l, axis=1), old)
            for c, l, old in zip(chunk, lane, carry)
        )

    carry = tuple(jnp.zeros((8, LANES), F32) for _ in range(blocks))
    for number in range(own_chunks):
        carry = found(rows_ref[number], number, carry)
    def reach(slot, carry):
        for part in range(per):
            carry = found(near_ref[slot, part], own_chunks + slot * per + part, carry)
        return carry

    bounds = []
    for axis, size in zip(AXES, sizes):
        at = lax.axis_index(axis)
        bounds.append((jnp.where(at > 0, 0, 1), jnp.where(at < size - 1, 3, 2)))
    (low_x, high_x), (low_y, high_y), (low_z, high_z) = bounds
    wide_y, wide_z = high_y - low_y, high_z - low_z

    def visit(step, carry):
        number = (low_x + step // (wide_y * wide_z)) * 9
        number = number + (low_y + step // wide_z % wide_y) * 3 + low_z + step % wide_z
        return reach(number, carry)

    carry = lax.fori_loop(0, (high_x - low_x) * wide_y * wide_z, visit, carry)
    for b, value in enumerate(carry):
        member_ref[b] = value

    def bunch(number, carry):
        names = [order_ref[number * TOGETHER + g] for g in range(TOGETHER)]
        counts = [steps_ref[name] for name in names]
        most = counts[-1]
        data = []
        state = []
        for name, n in zip(names, counts):
            value = member_ref[name]
            middle = jnp.sum(value[0:6], axis=1, keepdims=True) * (1.0 / length)
            moved = value[0:6] - middle
            mass = value[6:7]
            steps = jnp.full((3, LANES), n, jnp.int32)
            width = TIME_STEP / jnp.maximum(steps.astype(F32), 1.0)
            drift = jnp.broadcast_to(middle[3:6], (3, LANES)) * TIME_STEP
            data.append((mass, steps, width, drift, moved))
            position, velocity = moved[0:3], moved[3:6]
            state.append((position, velocity, *forces(position, velocity, mass)))

        def advance(step, state):
            after = []
            for (mass, steps, width, drift, moved), (position, velocity, acc, jerk) in zip(data, state):
                squared = width * width
                predicted = (
                    position + width * velocity + 0.5 * squared * acc + squared * width * (1.0 / 6.0) * jerk
                )
                predicted_vel = velocity + width * acc + 0.5 * squared * jerk
                acc_new, jerk_new = forces(predicted, predicted_vel, mass)
                velocity_new = (
                    velocity + 0.5 * width * (acc + acc_new) + squared * (1.0 / 12.0) * (jerk - jerk_new)
                )
                position_new = (
                    position + 0.5 * width * (velocity + velocity_new) + squared * (1.0 / 12.0) * (acc - acc_new)
                )
                live = steps > step
                after.append(
                    tuple(
                        jnp.where(live, new, old)
                        for new, old in (
                            (position_new, position), (velocity_new, velocity), (acc_new, acc), (jerk_new, jerk),
                        )
                    )
                )
            return tuple(after)

        state = lax.fori_loop(0, most, advance, tuple(state))
        for name, (mass, steps, width, drift, moved), (position, velocity, acc, jerk) in zip(names, data, state):
            change = jnp.concatenate([position - moved[0:3] + drift, velocity - moved[3:6]], axis=0)
            at = pl.multiple_of(slot_ref[name] * length, length)
            out_ref[:, pl.ds(at, length)] = change
        return carry

    lax.fori_loop(0, blocks // TOGETHER, bunch, 0)


def deliver(lanes, packed_ref, pos_ref, every_ref, out_ref, far_ref, own_sem, sems):
    here = tuple(lax.axis_index(axis) for axis in AXES)
    me = here[2]
    part = packed_ref.shape[1] // lanes
    barrier = pltpu.get_barrier_semaphore()

    def columns(number):
        return pl.ds(pl.multiple_of(number * part, LANES), part)

    own = pltpu.make_async_copy(packed_ref.at[:, columns(me)], out_ref.at[:, columns(me)], own_sem)
    own.start()

    def other(step):
        there = lax.rem(me + step, lanes)
        return there, (here[0], here[1], there)

    def greet(step, carry):
        pl.semaphore_signal(barrier, inc=1, device_id=other(step)[1], device_id_type=MESH)
        return carry

    lax.fori_loop(1, lanes, greet, 0)
    pl.semaphore_wait(barrier, lanes - 1)

    def send(step, carry):
        there, device = other(step)
        pltpu.make_async_remote_copy(
            src_ref=packed_ref.at[:, columns(there)],
            dst_ref=out_ref.at[:, columns(me)],
            send_sem=sems.at[0],
            recv_sem=sems.at[1],
            device_id=device,
            device_id_type=MESH,
        ).start()
        return carry

    lax.fori_loop(1, lanes, send, 0)
    far_field(pos_ref, every_ref, far_ref)
    own.wait()
    rest = packed_ref.at[:, pl.ds(0, (lanes - 1) * part)]
    pltpu.make_async_copy(rest, rest, sems.at[0]).wait()
    pltpu.make_async_copy(rest, rest, sems.at[1]).wait()


def finish(far_ref, arrived_ref, far_out_ref, out_ref, sems):
    first = pltpu.make_async_copy(arrived_ref, out_ref, sems.at[0])
    second = pltpu.make_async_copy(far_ref, far_out_ref, sems.at[1])
    first.start()
    second.start()
    first.wait()
    second.wait()


def vmem(count):
    return [pl.BlockSpec(memory_space=pltpu.VMEM)] * count


def on_device(
    sizes, positions, velocities, star_mass, far_previous, cell_index, ghost_list, block_index, block_owner, substeps
):
    lanes = sizes[2]
    domains = sizes[0] * sizes[1] * sizes[2]
    blocks, length = block_index.shape
    capacity = max(2, 2 * BLOCKS_DEV // lanes)
    stars, ghosts = positions.shape[1], ghost_list.shape[0]
    shape = jax.ShapeDtypeStruct
    sent = (ghosts // LANES, 8, LANES)
    rows, near, every = pl.pallas_call(
        functools.partial(exchange, sizes),
        out_shape=(
            shape((stars // LANES, 8, LANES), F32),
            shape((27, *sent), F32),
            shape((domains, 1, LANES), F32),
        ),
        in_specs=vmem(6),
        out_specs=tuple(vmem(3)),
        scratch_shapes=[
            pltpu.VMEM(sent, F32),
            pltpu.VMEM((1, 1, LANES), F32),
            pltpu.SemaphoreType.DMA,
            pltpu.SemaphoreType.DMA((2,)),
            pltpu.SemaphoreType.DMA((27,)),
            pltpu.SemaphoreType.DMA((27,)),
        ],
        compiler_params=pltpu.CompilerParams(collective_id=0, has_side_effects=True),
        name="exchange",
    )(
        positions,
        velocities,
        star_mass.reshape(1, stars),
        far_previous,
        cell_index.reshape(1, stars),
        ghost_list.reshape(1, ghosts),
    )
    smem = pl.BlockSpec(memory_space=pltpu.SMEM)
    packed = pl.pallas_call(
        functools.partial(step_stars, sizes, capacity),
        out_shape=shape((6, lanes * capacity * length), F32),
        in_specs=[smem, smem, *vmem(3)],
        out_specs=vmem(1)[0],
        scratch_shapes=[
            pltpu.VMEM((blocks, 8, LANES), F32),
            pltpu.SMEM((blocks,), jnp.int32),
            pltpu.SMEM((blocks,), jnp.int32),
        ],
        name="step_stars",
    )(substeps, block_owner.reshape(blocks), rows, near, block_index)
    arrived, far_acc = pl.pallas_call(
        functools.partial(deliver, lanes),
        out_shape=(shape(packed.shape, F32), shape((3, stars), F32)),
        in_specs=vmem(3),
        out_specs=tuple(vmem(2)),
        scratch_shapes=[pltpu.SemaphoreType.DMA, pltpu.SemaphoreType.DMA((2,))],
        compiler_params=pltpu.CompilerParams(collective_id=1, has_side_effects=True),
        name="deliver",
    )(packed, positions, every.reshape(domains, LANES))
    return pl.pallas_call(
        finish,
        out_shape=(shape(far_acc.shape, F32), shape(arrived.shape, F32)),
        in_specs=vmem(2),
        out_specs=(pl.BlockSpec(memory_space=pl.ANY), pl.BlockSpec(memory_space=pl.ANY)),
        scratch_shapes=[pltpu.SemaphoreType.DMA((2,))],
        name="finish",
    )(far_acc, arrived)


def solution(mesh):
    split = P(AXES)
    wide = P(None, AXES)
    tall = P(AXES, None)
    return jax.shard_map(
        functools.partial(on_device, tuple(mesh.shape[axis] for axis in AXES)),
        mesh=mesh,
        in_specs=(wide, wide, split, wide, split, split, tall, tall, split),
        out_specs=(wide, wide),
        check_vma=False,
    )
```

```python
import functools

import jax
import jax.numpy as jnp
from jax import lax
from jax.experimental import pallas as pl
from jax.experimental.pallas import tpu as pltpu
from jax.sharding import PartitionSpec as P

CELLS = 16
BLOCKS_DEV = 16
SUBMAX = 8
AXES = ("gx", "gy", "gz")
MESH = pl.DeviceIdType.MESH
LANES = 128

SOFTENING = 0.0025
INNER_RADIUS = 0.25
OUTER_RADIUS = 1.0
TIME_STEP = 0.25
SPAN = OUTER_RADIUS - INNER_RADIUS

BF16 = jnp.bfloat16
F32 = jnp.float32


def three(value):
    high = value.astype(BF16).astype(F32)
    rest = value - high
    middle = rest.astype(BF16).astype(F32)
    low = (rest - middle).astype(BF16).astype(F32)
    return high, middle, low


def pick(chunks, index):
    index = jnp.broadcast_to(index, (8, LANES))
    lane, chunk = index & (LANES - 1), index >> 7
    found = jnp.zeros((8, LANES), F32)
    for number, piece in chunks:
        found = jnp.where(chunk == number, jnp.take_along_axis(piece, lane, axis=1), found)
    return found


def prepare(pos_ref, vel_ref, mass_ref, far_ref, cell_ref, ghost_ref, rows_ref, sent_ref, moment_ref):
    stars = pos_ref.shape[1]
    position, mass = pos_ref[...], mass_ref[...]
    kicked = vel_ref[...] + far_ref[...] * (0.5 * TIME_STEP)
    rows = jnp.concatenate([position, kicked, mass, jnp.zeros((1, stars), F32)], axis=0)
    chunks = []
    for number in range(stars // LANES):
        piece = rows[:, number * LANES : (number + 1) * LANES]
        rows_ref[number] = piece
        chunks.append((number, piece))
    for number in range(ghost_ref.shape[1] // LANES):
        sent_ref[number] = pick(chunks, ghost_ref[:, number * LANES : (number + 1) * LANES])
    cell = lax.broadcasted_iota(jnp.int32, (LANES, stars), 0)
    member = jnp.where(jnp.broadcast_to(cell_ref[...], (LANES, stars)) == cell, 1.0, 0.0).astype(BF16)
    weighted = jnp.concatenate([mass, position * mass, jnp.zeros((4, stars), F32)], axis=0)
    parts = jnp.concatenate([*three(weighted), jnp.zeros_like(weighted)], axis=0).astype(BF16)
    sums = lax.dot_general(parts, member, (((1,), (1,)), ((), ())), preferred_element_type=F32)
    sums = sums[0:8] + sums[8:16] + sums[16:24]
    inside = lax.broadcasted_iota(jnp.int32, (1, LANES), 1) < CELLS
    total = jnp.where(inside, sums[0:1], 0.0)
    packed = total
    for axis in range(3):
        centre = jnp.where(inside, sums[axis + 1 : axis + 2] / jnp.where(inside, total, 1.0), 0.0)
        packed = packed + pltpu.roll(centre, (axis + 1) * CELLS, 1)
    moment_ref[0] = packed


def exchange(
    sizes, pos_ref, vel_ref, mass_ref, far_ref, cell_ref, ghost_ref, rows_ref, near_ref, every_ref,
    sent_ref, moment_ref, own_sem, moment_sems, send_sems, recv_sems,
):
    count = sizes[0] * sizes[1] * sizes[2]
    here = tuple(lax.axis_index(axis) for axis in AXES)
    barrier = pltpu.get_barrier_semaphore()

    turned = [[lax.rem(at + k, size) for k in range(size)] for at, size in zip(here[:2], sizes)]
    few = sizes[2] <= 4

    def each(act):
        for x, at_x in enumerate(turned[0]):
            for y, at_y in enumerate(turned[1]):
                first = 1 if x == 0 and y == 0 else 0

                def one(z, carry):
                    act((x * sizes[1] + y) * sizes[2] + z, (at_x, at_y, lax.rem(here[2] + z, sizes[2])))
                    return carry

                if few:
                    for z in range(first, sizes[2]):
                        one(z, 0)
                else:
                    lax.fori_loop(first, sizes[2], one, 0)

    each(lambda slot, device: pl.semaphore_signal(barrier, inc=1, device_id=device, device_id_type=MESH))
    prepare(pos_ref, vel_ref, mass_ref, far_ref, cell_ref, ghost_ref, rows_ref, sent_ref, moment_ref)
    own = pltpu.make_async_copy(moment_ref.at[0], every_ref.at[0], own_sem)
    own.start()
    pl.semaphore_wait(barrier, count - 1)

    def around(number):
        offset = (number // 9 - 1, number // 3 % 3 - 1, number % 3 - 1)
        there = tuple(a + b for a, b in zip(here, offset))
        inside = functools.reduce(
            jnp.logical_and, [(a >= 0) & (a < size) for a, size in zip(there, sizes)]
        )
        return there, inside

    def copy(number, there):
        return pltpu.make_async_remote_copy(
            src_ref=sent_ref,
            dst_ref=near_ref.at[26 - number],
            send_sem=send_sems.at[number],
            recv_sem=recv_sems.at[26 - number],
            device_id=there,
            device_id_type=MESH,
        )

    for number in range(27):
        if number != 13:
            there, inside = around(number)

            @pl.when(inside)
            def _():
                copy(number, there).start()

    def share(slot, device):
        pltpu.make_async_remote_copy(
            src_ref=moment_ref.at[0],
            dst_ref=every_ref.at[slot],
            send_sem=moment_sems.at[0],
            recv_sem=moment_sems.at[1],
            device_id=device,
            device_id_type=MESH,
        ).start()

    each(share)
    own.wait()
    rest = every_ref.at[pl.ds(1, count - 1)]
    pltpu.make_async_copy(rest, rest, moment_sems.at[0]).wait()
    pltpu.make_async_copy(rest, rest, moment_sems.at[1]).wait()
    for number in range(27):
        if number != 13:
            there, inside = around(number)

            @pl.when(inside)
            def _():
                pltpu.make_async_copy(sent_ref, sent_ref, send_sems.at[number]).wait()
                pltpu.make_async_copy(near_ref.at[number], near_ref.at[number], recv_sems.at[number]).wait()


def forces(position, velocity, mass):
    norm = jnp.sum(position * position, axis=0, keepdims=True) + 0.5 * SOFTENING
    mixed = jnp.sum(position * velocity, axis=0, keepdims=True)
    nought = jnp.zeros((2, LANES), F32)
    row = lax.broadcasted_iota(jnp.int32, (8, LANES), 0)
    state_row, norm_row, mixed_row = row < 6, row == 6, row == 7
    norm_one, mixed_one = jnp.where(norm_row, 1.0, 0.0), jnp.where(mixed_row, 1.0, 0.0)
    scale = jnp.where(row < 3, -2.0, 0.0)
    left = jnp.concatenate([position, velocity, norm, mixed], axis=0)
    high, middle, low = three(left)
    high_one, middle_one = jnp.where(state_row, high, 1.0), jnp.where(state_row, middle, 1.0)
    left_all = jnp.concatenate([high, high_one, high_one, middle, middle_one, low], axis=0)
    turn = three(jnp.concatenate([-velocity, -position, nought], axis=0))

    def right(parts, mine, one):
        first = jnp.where(mine, one, parts[0])
        second = jnp.where(mine, high, parts[1])
        third = jnp.where(mine, middle, parts[2])
        fourth = jnp.where(mine, low, parts[1])
        return jnp.concatenate([first, second, third, first, fourth, first], axis=0)

    right_all = jnp.concatenate(
        [right((high * scale, middle * scale, low * scale), norm_row, norm_one), right(turn, mixed_row, mixed_one)],
        axis=1,
    )
    pairs = lax.dot_general(
        left_all.astype(BF16),
        right_all.astype(BF16),
        (((0,), (0,)), ((), ())),
        preferred_element_type=F32,
    )
    square, rate = pairs[:, 0:LANES], pairs[:, LANES:]
    inverse = lax.rsqrt(square)
    radius = square * inverse
    inverse2 = inverse * inverse
    near = jnp.clip(OUTER_RADIUS / SPAN - radius * (1.0 / SPAN), 0.0, 1.0)
    weight = (near * near) * (3.0 - 2.0 * near) * (inverse * inverse2)
    turned = weight * (rate * inverse2)
    weight_h = weight.astype(BF16)
    weight_l = (weight - weight_h.astype(F32)).astype(BF16)
    turned_h = turned.astype(BF16)
    turned_l = (turned - turned_h.astype(F32)).astype(BF16)
    matrix = jnp.concatenate(
        [
            jnp.concatenate([weight_h, turned_h], axis=1),
            jnp.concatenate([weight_l, turned_l], axis=1),
        ],
        axis=0,
    )
    values = jnp.where(state_row, left, norm_one) * mass
    values = jnp.concatenate([*three(values), jnp.zeros_like(values)], axis=0).astype(BF16)
    sums = jnp.dot(jnp.concatenate([values, values], axis=1), matrix, preferred_element_type=F32)
    sums = sums[0:8] + sums[8:16] + sums[16:24]
    plain, bent = sums[:, 0:LANES], sums[:, LANES:]
    acceleration = plain[0:3] - position * plain[6:7]
    jerk = plain[3:6] - velocity * plain[6:7] - 3.0 * (bent[0:3] - position * bent[6:7])
    return acceleration, jerk


def far_field(pos_ref, every_ref, far_ref):
    stars = pos_ref.shape[1]
    domains = every_ref.shape[0]
    group = min(32, domains)

    def chunk(number, carry):
        columns = pl.ds(pl.multiple_of(number * LANES, LANES), LANES)
        star = [jnp.broadcast_to(pos_ref[axis : axis + 1, columns], (CELLS, LANES)) for axis in range(3)]

        def some(step, total):
            rows = every_ref[pl.ds(pl.multiple_of(step * group, group), group), :]
            table = rows.T
            for k in range(group):
                mass, *centre = [
                    jnp.broadcast_to(table[c * CELLS : (c + 1) * CELLS, k : k + 1], (CELLS, LANES))
                    for c in range(4)
                ]
                offset = [c - s for c, s in zip(centre, star)]
                square = offset[0] * offset[0] + offset[1] * offset[1] + offset[2] * offset[2] + SOFTENING
                inverse = lax.rsqrt(square)
                fraction = jnp.clip(square * inverse * (1.0 / SPAN) - INNER_RADIUS / SPAN, 0.0, 1.0)
                weight = mass * (fraction * fraction * (3.0 - 2.0 * fraction)) * (inverse * inverse * inverse)
                total = tuple(t + weight * o for t, o in zip(total, offset))
            return total

        total = lax.fori_loop(
            0, domains // group, some, tuple(jnp.zeros((CELLS, LANES), F32) for _ in range(3))
        )
        far_ref[:, columns] = jnp.concatenate([jnp.sum(t, axis=0, keepdims=True) for t in total], axis=0)
        return carry

    lax.fori_loop(0, stars // LANES, chunk, 0)


TOGETHER = 8


def step_stars(
    sizes, capacity, steps_ref, owner_ref, rows_ref, near_ref, index_ref, out_ref, member_ref, slot_ref, order_ref,
):
    blocks, length = index_ref.shape
    out_ref[...] = jnp.zeros_like(out_ref)

    counts = [steps_ref[b] for b in range(blocks)]
    owners = [owner_ref[b] for b in range(blocks)]
    places = [jnp.int32(0)] * blocks
    for b in range(blocks):
        rank = jnp.int32(0)
        for earlier in range(b):
            before = (counts[earlier] <= counts[b]).astype(jnp.int32)
            places[b] = places[b] + before
            places[earlier] = places[earlier] + (1 - before)
            rank = rank + (owners[earlier] == owners[b]).astype(jnp.int32)
        slot_ref[b] = owners[b] * capacity + rank
    for b in range(blocks):
        order_ref[places[b]] = b

    own_chunks = rows_ref.shape[0]
    per = near_ref.shape[1]
    indices = [jnp.broadcast_to(index_ref[b : b + 1, :], (8, LANES)) for b in range(blocks)]
    lane = [i & (LANES - 1) for i in indices]
    chunk = [i >> 7 for i in indices]

    def found(piece, number, carry):
        return tuple(
            jnp.where(c == number, jnp.take_along_axis(piece, l, axis=1), old)
            for c, l, old in zip(chunk, lane, carry)
        )

    carry = tuple(jnp.zeros((8, LANES), F32) for _ in range(blocks))
    for number in range(own_chunks):
        carry = found(rows_ref[number], number, carry)
    def reach(slot, carry):
        for part in range(per):
            carry = found(near_ref[slot, part], own_chunks + slot * per + part, carry)
        return carry

    bounds = []
    for axis, size in zip(AXES, sizes):
        at = lax.axis_index(axis)
        bounds.append((jnp.where(at > 0, 0, 1), jnp.where(at < size - 1, 3, 2)))
    (low_x, high_x), (low_y, high_y), (low_z, high_z) = bounds
    wide_y, wide_z = high_y - low_y, high_z - low_z

    def visit(step, carry):
        number = (low_x + step // (wide_y * wide_z)) * 9
        number = number + (low_y + step // wide_z % wide_y) * 3 + low_z + step % wide_z
        return reach(number, carry)

    carry = lax.fori_loop(0, (high_x - low_x) * wide_y * wide_z, visit, carry)
    for b, value in enumerate(carry):
        member_ref[b] = value

    def bunch(number, carry):
        names = [order_ref[number * TOGETHER + g] for g in range(TOGETHER)]
        counts = [steps_ref[name] for name in names]
        most = counts[-1]
        data = []
        state = []
        for name, n in zip(names, counts):
            value = member_ref[name]
            middle = jnp.sum(value[0:6], axis=1, keepdims=True) * (1.0 / length)
            moved = value[0:6] - middle
            mass = value[6:7]
            steps = jnp.full((3, LANES), n, jnp.int32)
            width = TIME_STEP / jnp.maximum(steps.astype(F32), 1.0)
            drift = jnp.broadcast_to(middle[3:6], (3, LANES)) * TIME_STEP
            data.append((mass, steps, width, drift, moved))
            position, velocity = moved[0:3], moved[3:6]
            state.append((position, velocity, *forces(position, velocity, mass)))

        def advance(step, state):
            after = []
            for (mass, steps, width, drift, moved), (position, velocity, acc, jerk) in zip(data, state):
                squared = width * width
                predicted = (
                    position + width * velocity + 0.5 * squared * acc + squared * width * (1.0 / 6.0) * jerk
                )
                predicted_vel = velocity + width * acc + 0.5 * squared * jerk
                acc_new, jerk_new = forces(predicted, predicted_vel, mass)
                velocity_new = (
                    velocity + 0.5 * width * (acc + acc_new) + squared * (1.0 / 12.0) * (jerk - jerk_new)
                )
                position_new = (
                    position + 0.5 * width * (velocity + velocity_new) + squared * (1.0 / 12.0) * (acc - acc_new)
                )
                live = steps > step
                after.append(
                    tuple(
                        jnp.where(live, new, old)
                        for new, old in (
                            (position_new, position), (velocity_new, velocity), (acc_new, acc), (jerk_new, jerk),
                        )
                    )
                )
            return tuple(after)

        state = lax.fori_loop(0, most, advance, tuple(state))
        for name, (mass, steps, width, drift, moved), (position, velocity, acc, jerk) in zip(names, data, state):
            change = jnp.concatenate([position - moved[0:3] + drift, velocity - moved[3:6]], axis=0)
            at = pl.multiple_of(slot_ref[name] * length, length)
            out_ref[:, pl.ds(at, length)] = change
        return carry

    lax.fori_loop(0, blocks // TOGETHER, bunch, 0)


def deliver(lanes, packed_ref, pos_ref, every_ref, out_ref, far_ref, own_sem, sems):
    here = tuple(lax.axis_index(axis) for axis in AXES)
    me = here[2]
    part = packed_ref.shape[1] // lanes
    barrier = pltpu.get_barrier_semaphore()

    def columns(number):
        return pl.ds(pl.multiple_of(number * part, LANES), part)

    own = pltpu.make_async_copy(packed_ref.at[:, columns(me)], out_ref.at[:, columns(me)], own_sem)
    own.start()

    def other(step):
        there = lax.rem(me + step, lanes)
        return there, (here[0], here[1], there)

    def greet(step, carry):
        pl.semaphore_signal(barrier, inc=1, device_id=other(step)[1], device_id_type=MESH)
        return carry

    lax.fori_loop(1, lanes, greet, 0)
    pl.semaphore_wait(barrier, lanes - 1)

    def send(step, carry):
        there, device = other(step)
        pltpu.make_async_remote_copy(
            src_ref=packed_ref.at[:, columns(there)],
            dst_ref=out_ref.at[:, columns(me)],
            send_sem=sems.at[0],
            recv_sem=sems.at[1],
            device_id=device,
            device_id_type=MESH,
        ).start()
        return carry

    lax.fori_loop(1, lanes, send, 0)
    far_field(pos_ref, every_ref, far_ref)
    own.wait()
    rest = packed_ref.at[:, pl.ds(0, (lanes - 1) * part)]
    pltpu.make_async_copy(rest, rest, sems.at[0]).wait()
    pltpu.make_async_copy(rest, rest, sems.at[1]).wait()


def finish(far_ref, arrived_ref, far_out_ref, out_ref, sems):
    first = pltpu.make_async_copy(arrived_ref, out_ref, sems.at[0])
    second = pltpu.make_async_copy(far_ref, far_out_ref, sems.at[1])
    first.start()
    second.start()
    first.wait()
    second.wait()


def vmem(count):
    return [pl.BlockSpec(memory_space=pltpu.VMEM)] * count


def on_device(
    sizes, positions, velocities, star_mass, far_previous, cell_index, ghost_list, block_index, block_owner, substeps
):
    lanes = sizes[2]
    domains = sizes[0] * sizes[1] * sizes[2]
    blocks, length = block_index.shape
    capacity = max(2, 2 * BLOCKS_DEV // lanes)
    stars, ghosts = positions.shape[1], ghost_list.shape[0]
    shape = jax.ShapeDtypeStruct
    sent = (ghosts // LANES, 8, LANES)
    rows, near, every = pl.pallas_call(
        functools.partial(exchange, sizes),
        out_shape=(
            shape((stars // LANES, 8, LANES), F32),
            shape((27, *sent), F32),
            shape((domains, 1, LANES), F32),
        ),
        in_specs=vmem(6),
        out_specs=tuple(vmem(3)),
        scratch_shapes=[
            pltpu.VMEM(sent, F32),
            pltpu.VMEM((1, 1, LANES), F32),
            pltpu.SemaphoreType.DMA,
            pltpu.SemaphoreType.DMA((2,)),
            pltpu.SemaphoreType.DMA((27,)),
            pltpu.SemaphoreType.DMA((27,)),
        ],
        compiler_params=pltpu.CompilerParams(collective_id=0, has_side_effects=True),
        name="exchange",
    )(
        positions,
        velocities,
        star_mass.reshape(1, stars),
        far_previous,
        cell_index.reshape(1, stars),
        ghost_list.reshape(1, ghosts),
    )
    smem = pl.BlockSpec(memory_space=pltpu.SMEM)
    packed = pl.pallas_call(
        functools.partial(step_stars, sizes, capacity),
        out_shape=shape((6, lanes * capacity * length), F32),
        in_specs=[smem, smem, *vmem(3)],
        out_specs=vmem(1)[0],
        scratch_shapes=[
            pltpu.VMEM((blocks, 8, LANES), F32),
            pltpu.SMEM((blocks,), jnp.int32),
            pltpu.SMEM((blocks,), jnp.int32),
        ],
        name="step_stars",
    )(substeps, block_owner.reshape(blocks), rows, near, block_index)
    arrived, far_acc = pl.pallas_call(
        functools.partial(deliver, lanes),
        out_shape=(shape(packed.shape, F32), shape((3, stars), F32)),
        in_specs=vmem(3),
        out_specs=tuple(vmem(2)),
        scratch_shapes=[pltpu.SemaphoreType.DMA, pltpu.SemaphoreType.DMA((2,))],
        compiler_params=pltpu.CompilerParams(collective_id=1, has_side_effects=True),
        name="deliver",
    )(packed, positions, every.reshape(domains, LANES))
    return pl.pallas_call(
        finish,
        out_shape=(shape(far_acc.shape, F32), shape(arrived.shape, F32)),
        in_specs=vmem(2),
        out_specs=(pl.BlockSpec(memory_space=pl.ANY), pl.BlockSpec(memory_space=pl.ANY)),
        scratch_shapes=[pltpu.SemaphoreType.DMA((2,))],
        name="finish",
    )(far_acc, arrived)


def solution(mesh):
    split = P(AXES)
    wide = P(None, AXES)
    tall = P(AXES, None)
    return jax.shard_map(
        functools.partial(on_device, tuple(mesh.shape[axis] for axis in AXES)),
        mesh=mesh,
        in_specs=(wide, wide, split, wide, split, split, tall, tall, split),
        out_specs=(wide, wide),
        check_vma=False,
    )
```
